128 devices in a mesh: gz: 32 (over y, z, core), phi: 4 (over x).
Axes of the slice: x: 4, y: 4, z: 4, core: 2. Of those that a mesh axis runs over, the one named last changes fastest.
Arguments:
- field: float32 [16, 4, 2048, 1024], P(None, None, 'gz', 'phi'), may hold values from -6 to 6
- field_tangent: float32 [16, 4, 2048, 1024], P(None, None, 'gz', 'phi'), may hold values from -6 to 6
- spectral_weight: float32 [2, 16, 16, 64, 64], P(None, None, None, 'gz', 'phi'), may hold values from -1 to 1
- local_weight: float32 [16, 16], replicated, may hold values from -1.5 to 1.5
- bias_term: float32 [16], replicated, may hold values from -3 to 3
- z_modes: int32 [64], replicated, may hold values from 0 to 1023, as said below
- phi_modes: int32 [64], replicated, may hold values from 0 to 1023, as said below
Outputs:
- output: float32 [16, 4, 2048, 1024], P(None, None, 'gz', 'phi')
- output_tangent: float32 [16, 4, 2048, 1024], P(None, None, 'gz', 'phi')
The draws below stay inside these ranges and needn't reach their ends.
Inputs may be any that keep to these rules, and one draw needn't show every extreme that they name: `z_modes`: entries may repeat; 0 and 1023 both occur. `phi_modes`: entries may repeat; 0 and 1023 both occur.
All inputs are finite; a program needn't handle non-finite values.
Results may differ from the reference program's by a relative error of at most 0.000078.
Values sent between devices are 32-bit elements; how exact they have to be, the bound alone decides.
A program may use at most 128 MiB of HBM per device.

```python
import functools
import math
import jax
import jax.numpy as jnp
from jax import lax

C = 16
CYCLE = 4
Z = 2048
PHI = 1024
KZ = 64
KP = 64


def place_ends(key, count, upper):
    values = jax.random.randint(key, (count,), 0, upper, dtype=jnp.int32)
    slots = jax.random.permutation(jax.random.fold_in(key, 7), count)
    return values.at[slots[0]].set(0).at[slots[1]].set(upper - 1)


def draw_z_modes(key, part):
    return place_ends(jax.random.fold_in(key, 11), KZ, Z // 2)


def draw_phi_modes(key, part):
    return place_ends(jax.random.fold_in(key, 13), KP, PHI)


def level_of(stream_key, dims, shards, low, largest):
    level = 1.0
    for axis_at, shards_of in shards:
        heights = jax.random.uniform(jax.random.fold_in(jax.random.fold_in(stream_key, 6), axis_at), (shards_of,), jnp.float32, low / len(shards), largest / len(shards))
        level = level * jnp.repeat(jnp.exp(heights), dims[axis_at] // shards_of).reshape((-1,) + (1,) * (len(dims) - 1 - axis_at))
    return level


def gaussian(stream_key, extent, spread, limit, pieces=(), kind=jnp.bfloat16):
    values = spread * jax.random.normal(stream_key, extent, jnp.float32)
    if pieces:
        values = values * level_of(stream_key, extent, pieces, -0.22, 0.18)
    return jnp.clip(values, -limit, limit).astype(kind)


def setup_inputs(seed: int = 0) -> dict:
    keys = jax.random.split(jax.random.key(seed), 8)
    return {
        "field": gaussian(keys[0], (C, CYCLE, Z, PHI), 1.0, 6.0, ((2, 32), (3, 4)), jnp.float32),
        "field_tangent": gaussian(keys[1], (C, CYCLE, Z, PHI), 1.0, 6.0, ((2, 32), (3, 4)), jnp.float32),
        "spectral_weight": gaussian(keys[2], (2, C, C, KZ, KP), (2 * C) ** -0.5, 1.0, ((3, 32), (4, 4)), jnp.float32),
        "local_weight": gaussian(keys[3], (C, C), C ** -0.5, 1.5, (), jnp.float32),
        "bias_term": gaussian(keys[4], (C,), 0.5, 3.0, (), jnp.float32),
        "z_modes": draw_z_modes(jax.random.fold_in(keys[7], 71), 0),
        "phi_modes": draw_phi_modes(jax.random.fold_in(keys[7], 71), 0),
    }


precise = lax.Precision.HIGHEST

def angle_table(positions, modes, length):
    product = positions[:, None] * modes[None, :] % length
    angle = product.astype(jnp.float32) * (2.0 * math.pi / length)
    return (jnp.cos(angle), jnp.sin(angle))

def cycle_layer(stacked, spectral_weight, local_weight, bias_term, z_modes, phi_modes):
    z_cosine, z_sine = angle_table(jnp.arange(Z, dtype=jnp.int32), z_modes, Z)
    p_cosine, p_sine = angle_table(jnp.arange(PHI, dtype=jnp.int32), phi_modes, PHI)
    zreal = jnp.einsum('pczf,zk->pckf', stacked, z_cosine, precision=precise)
    zimag = -jnp.einsum('pczf,zk->pckf', stacked, z_sine, precision=precise)
    scaling = 1.0 / math.sqrt(Z * PHI)
    freal = (jnp.einsum('pckf,fq->pckq', zreal, p_cosine, precision=precise) + jnp.einsum('pckf,fq->pckq', zimag, p_sine, precision=precise)) * scaling
    fimag = (jnp.einsum('pckf,fq->pckq', zimag, p_cosine, precision=precise) - jnp.einsum('pckf,fq->pckq', zreal, p_sine, precision=precise)) * scaling
    wreal = spectral_weight[0]
    wimag = spectral_weight[1]
    greal = jnp.einsum('pckq,cokq->pokq', freal, wreal, precision=precise) - jnp.einsum('pckq,cokq->pokq', fimag, wimag, precision=precise)
    gimag = jnp.einsum('pckq,cokq->pokq', fimag, wreal, precision=precise) + jnp.einsum('pckq,cokq->pokq', freal, wimag, precision=precise)
    hreal = jnp.einsum('pokq,fq->pokf', greal, p_cosine, precision=precise) - jnp.einsum('pokq,fq->pokf', gimag, p_sine, precision=precise)
    himag = jnp.einsum('pokq,fq->pokf', greal, p_sine, precision=precise) + jnp.einsum('pokq,fq->pokf', gimag, p_cosine, precision=precise)
    spectral = (jnp.einsum('pokf,zk->pozf', hreal, z_cosine, precision=precise) - jnp.einsum('pokf,zk->pozf', himag, z_sine, precision=precise)) * (2.0 / math.sqrt(KZ * KP))
    mixing = jnp.einsum('pczf,co->pozf', stacked, local_weight, precision=precise)
    preact = spectral[0] + mixing[0] + bias_term[:, None, None]
    tangent = spectral[1] + mixing[1]
    return jax.jvp(functools.partial(jax.nn.gelu, approximate=True), (preact,), (tangent,))

def reference(field, field_tangent, spectral_weight, local_weight, bias_term, z_modes, phi_modes):

    def one_cycle(index):
        stacked = jnp.stack([lax.dynamic_index_in_dim(field, index, 1, keepdims=False), lax.dynamic_index_in_dim(field_tangent, index, 1, keepdims=False)])
        return cycle_layer(stacked, spectral_weight, local_weight, bias_term, z_modes, phi_modes)
    output, output_tangent = lax.map(one_cycle, jnp.arange(CYCLE, dtype=jnp.int32))
    return (jnp.swapaxes(output, 0, 1), jnp.swapaxes(output_tangent, 0, 1))
```

```python
import functools
import math

import jax
import jax.numpy as jnp
from jax import lax
from jax.experimental import pallas as pl
from jax.experimental.pallas import tpu as pltpu
from jax.sharding import PartitionSpec as P

C, R, ZL, FL = 16, 4, 64, 256
Z, PHI, KZ, KP = 2048, 1024, 64, 64
F32, BF16, I32 = jnp.float32, jnp.bfloat16, jnp.int32
MESH = pl.DeviceIdType.MESH
SCALE = (1.0 / math.sqrt(Z * PHI)) * (2.0 / math.sqrt(KZ * KP))


def iota(shape, dim):
    return lax.broadcasted_iota(I32, shape, dim)


def split(x):
    hi = x.astype(BF16)
    return hi, (x - hi.astype(F32)).astype(BF16)


def wave(turns, length):
    return jnp.cos((turns & (length - 1)).astype(F32) * (2.0 * math.pi / length))


def nt(a, b):
    return lax.dot_general(a, b, (((1,), (1,)), ((), ())), preferred_element_type=F32)


def nn(a, b):
    return jnp.dot(a, b, preferred_element_type=F32)


def phi_table(pcol_ref):
    shape = (128, FL)
    f = lax.axis_index("phi") * FL + iota(shape, 1)
    return wave(f * pcol_ref[...] + (iota(shape, 0) // 64) * (PHI // 4), PHI)


def stack_z(x_refs, i):
    rows = pl.ds(i, 64, stride=8)
    a, b, c, d = (r.reshape(512, 128)[rows, :] for r in x_refs)
    return jnp.concatenate([jnp.concatenate([a, b], axis=1), jnp.concatenate([c, d], axis=1)], axis=0)


def halves():
    left = pl.BlockSpec((64, 8, 128), lambda j: (0, j, 0))
    right = pl.BlockSpec((64, 8, 128), lambda j: (0, j, 1))
    return [left, right, left, right]


def forward_kernel(xa_ref, xb_ref, xc_ref, xd_ref, pcol_ref, zcol_ref, s_ref, a_ref, w_ref):
    step = pl.program_id(0)

    @pl.when(step == 0)
    def _():
        hi, lo = split(phi_table(pcol_ref))
        w_ref[0:128, :] = hi
        w_ref[128:256, :] = lo

    for i in range(8):
        hi, lo = split(stack_z((xa_ref, xb_ref, xc_ref, xd_ref), i))
        o = nt(w_ref[...], jnp.concatenate([hi, lo], axis=0))
        r = o[:128, :128] + (o[:128, 128:] + o[128:, :128])
        a_ref[pl.ds(step * 8 + i, 128, stride=64), :] = r

    @pl.when(step == pl.num_programs(0) - 1)
    def _():
        shape = (128, 128)
        z = lax.axis_index("gz") * ZL + iota(shape, 1) % 64
        turn = (iota(shape, 0) % 2 - iota(shape, 1) // 64) * (Z // 4)
        t_hi, t_lo = split(wave(z * zcol_ref[...] + turn, Z))
        tt = jnp.concatenate([t_hi, t_lo], axis=1)

        def one(q, carry):
            q64 = pl.multiple_of(q * 64, 64)
            a = jnp.concatenate([a_ref[pl.ds(q64, 64), :], a_ref[pl.ds(4096 + q64, 64), :]], axis=0)
            hi, lo = split(a)
            top = jnp.concatenate([hi, lo], axis=1)
            low = jnp.concatenate([hi, jnp.zeros_like(lo)], axis=1)
            o = nn(tt, jnp.concatenate([top, low], axis=0))
            r = o[:, :128] + o[:, 128:]
            s_ref[pl.ds((q // 16) * 1024 + q % 16, 64, stride=16), :] = r[:64]
            s_ref[pl.ds(4096 + q, 64, stride=64), :] = r[64:]
            return carry

        lax.fori_loop(0, 64, one, 0, unroll=4)


def forward(field, field_tangent, pcol, zcol):
    whole = lambda shape: pl.BlockSpec(shape, lambda j: (0,) * len(shape))
    return pl.pallas_call(
        forward_kernel,
        grid=(8,),
        out_shape=jax.ShapeDtypeStruct((8192, 128), F32),
        in_specs=halves() + [whole((128, 1)), whole((128, 1))],
        out_specs=whole((8192, 128)),
        scratch_shapes=[pltpu.VMEM((8192, 128), F32), pltpu.VMEM((256, FL), BF16)],
        compiler_params=pltpu.CompilerParams(vmem_limit_bytes=40 << 20),
        name="forward_kernel",
    )(field, field, field_tangent, field_tangent, pcol, zcol)


def mix(x_ref, w_ref, out_ref):
    lane = iota((16, 128), 1) % 64
    for k in range(2):
        xr = x_ref[pl.ds(k * 32, 16), :]
        xi = x_ref[pl.ds(k * 32 + 16, 16), :]
        gr = jnp.zeros((16, 128), F32)
        gi = jnp.zeros((16, 128), F32)
        for d in range(16):
            if d == 0:
                ar, ai = xr, xi
            else:
                near = lane < 64 - 4 * d
                ar = jnp.where(near, pltpu.roll(xr, 128 - 4 * d, 1), pltpu.roll(xr, 64 - 4 * d, 1))
                ai = jnp.where(near, pltpu.roll(xi, 128 - 4 * d, 1), pltpu.roll(xi, 64 - 4 * d, 1))
            wr = w_ref[pl.ds(d * 64 + k * 16, 16), :]
            wi = w_ref[pl.ds(d * 64 + 32 + k * 16, 16), :]
            gr = gr + (ar * wr - ai * wi)
            gi = gi + (ai * wr + ar * wi)
        out_ref[pl.ds(k * 32, 16), :] = gr
        out_ref[pl.ds(k * 32 + 16, 16), :] = gi


def exchange_kernel(
    s_ref, w_ref, g_ref,
    part, peer, relay, fin, second, rec2, third, rec3, own, gath3, gath2,
    load_sem, pair_s, pair_r, st1_s, st1_r, st2_s, st2_r, st3_s, st3_r,
    ag3_s, ag3_r, ag2_s, ag2_r, ag1_s, ag1_r, out_s, out_r, keep_sem,
):
    gz = lax.axis_index("gz")
    x = lax.axis_index("phi")
    core = gz % 2
    z = (gz // 2) % 4
    y = gz // 8

    def device(xx, yy, zz, cc):
        return ((yy * 4 + zz) * 2 + cc, xx)

    pa = x + core * (y - x)
    pb = y + core * (z - y)
    pd = z + core * (x - z)

    def along_a(t):
        n = (pa + t) % 4
        return device(n + core * (x - n), y + core * (n - y), z, core)

    def along_b(t):
        n = (pb + t) % 4
        return device(x, n + core * (y - n), z + core * (n - z), core)

    def along_d(t):
        n = (pd + t) % 4
        return device(x + core * (n - x), y, n + core * (z - n), core)

    partner = device(x, y, z, 1 - core)

    def remote(src, dst, ss, rs, dev):
        return pltpu.make_async_remote_copy(
            src_ref=src, dst_ref=dst, send_sem=ss, recv_sem=rs, device_id=dev, device_id_type=MESH
        )

    barrier = pltpu.get_barrier_semaphore()
    peers = [partner, along_a(1), along_a(3)]
    peers += [along_b(t) for t in (1, 2, 3)] + [along_d(t) for t in (1, 2, 3)]
    for dev in peers:
        pl.semaphore_signal(barrier, inc=1, device_id=dev, device_id_type=MESH)

    def mine(t):
        return pl.multiple_of(((pa + t) % 4) * 1024, 1024)

    qa = y + core * (x - y)

    def theirs(t):
        return pl.multiple_of(((qa + t) % 4) * 1024, 1024)

    order = (2, 1, 3, 0)
    loads = []
    for n, t in enumerate(order):
        c = pltpu.make_async_copy(
            s_ref.at[pl.ds(pl.multiple_of(core * 4096, 1024) + mine(t), 1024), :], part.at[pl.ds(n * 1024, 1024), :], load_sem.at[n]
        )
        c.start()
        loads.append(c)
    pl.semaphore_wait(barrier, 9)
    pairs = []
    for n, t in enumerate(order):
        c = remote(
            s_ref.at[pl.ds(pl.multiple_of((1 - core) * 4096, 1024) + theirs(t), 1024), :],
            peer.at[pl.ds(n * 1024, 1024), :], pair_s.at[n], pair_r.at[n], partner,
        )
        c.start()
        pairs.append(c)

    def add_into(dst, src, d0, s0, rows):
        def one(i, carry):
            o = pl.multiple_of(i * 64, 64)
            dst[pl.ds(d0 + o, 64), :] = dst[pl.ds(d0 + o, 64), :] + src[pl.ds(s0 + o, 64), :]
            return carry

        lax.fori_loop(0, rows // 64, one, 0)

    def land(n):
        loads[n].wait()
        pairs[n].wait_recv()
        add_into(part, peer, n * 1024, n * 1024, 1024)

    land(0)
    right, left = along_a(1), along_a(3)
    relay_r = remote(part.at[pl.ds(0, 512), :], relay.at[pl.ds(0, 512), :], st1_s.at[0], st1_r.at[0], right)
    relay_l = remote(part.at[pl.ds(512, 512), :], relay.at[pl.ds(512, 512), :], st1_s.at[1], st1_r.at[1], left)
    relay_r.start()
    relay_l.start()
    land(1)
    own_r = remote(part.at[pl.ds(1024 + 512, 512), :], fin.at[pl.ds(512, 512), :], st1_s.at[2], st1_r.at[2], right)
    own_r.start()
    land(2)
    own_l = remote(part.at[pl.ds(2048, 512), :], fin.at[pl.ds(1024, 512), :], st1_s.at[3], st1_r.at[3], left)
    own_l.start()
    land(3)
    relay_r.wait_recv()
    add_into(part, relay, 1024, 0, 512)
    sum_r = remote(part.at[pl.ds(1024, 512), :], fin.at[pl.ds(0, 512), :], st1_s.at[4], st1_r.at[4], right)
    sum_r.start()
    relay_l.wait_recv()
    add_into(part, relay, 2048 + 512, 512, 512)
    sum_l = remote(part.at[pl.ds(2048 + 512, 512), :], fin.at[pl.ds(1536, 512), :], st1_s.at[5], st1_r.at[5], left)
    sum_l.start()
    own_r.wait_recv()
    own_l.wait_recv()
    sum_r.wait_recv()
    sum_l.wait_recv()

    def first_sum(i, carry):
        o = pl.multiple_of(i * 64, 64)
        second[pl.ds(o, 64), :] = part[pl.ds(3072 + o, 64), :] + (fin[pl.ds(o, 64), :] + fin[pl.ds(1024 + o, 64), :])
        return carry

    lax.fori_loop(0, 16, first_sum, 0)

    sends2 = []
    for t in (2, 1, 3):
        c = remote(
            second.at[pl.ds(pl.multiple_of(((pb + t) % 4) * 256, 256), 256), :],
            rec2.at[pl.ds((t - 1) * 256, 256), :], st2_s.at[t - 1], st2_r.at[t - 1], along_b(t),
        )
        c.start()
        sends2.append(c)
    for c in sends2:
        c.wait_recv()
    base2 = pl.multiple_of(pb * 256, 256)
    for i in range(4):
        for j in range(4):
            o = (i * 4 + j) * 16
            src = pl.multiple_of(o + core * ((j * 4 + i) * 16 - o), 16)
            v = second[pl.ds(base2 + src, 16), :] + rec2[pl.ds(src, 16), :]
            v = v + (rec2[pl.ds(256 + src, 16), :] + rec2[pl.ds(512 + src, 16), :])
            third[pl.ds(o, 16), :] = v

    sends3 = []
    for t in (2, 1, 3):
        c = remote(
            third.at[pl.ds(pl.multiple_of(((pd + t) % 4) * 64, 64), 64), :],
            rec3.at[pl.ds((t - 1) * 64, 64), :], st3_s.at[t - 1], st3_r.at[t - 1], along_d(t),
        )
        c.start()
        sends3.append(c)
    for c in sends3:
        c.wait_recv()
    own[...] = third[pl.ds(pl.multiple_of(pd * 64, 64), 64), :] + rec3[pl.ds(0, 64), :] + (
        rec3[pl.ds(64, 64), :] + rec3[pl.ds(128, 64), :]
    )
    mine3 = gath3.at[pl.ds(pl.multiple_of(pd * 64, 64), 64), :]
    mix(own, w_ref, mine3)

    gat3 = []
    for t in (2, 1, 3):
        c = remote(mine3, mine3, ag3_s.at[t - 1], ag3_r.at[t - 1], along_d(t))
        c.start()
        gat3.append(c)
    for c in gat3:
        c.wait_recv()
    for i in range(4):
        for j in range(4):
            o = (i * 4 + j) * 16
            src = pl.multiple_of(o + core * ((j * 4 + i) * 16 - o), 16)
            gath2[pl.ds(base2 + o, 16), :] = gath3[pl.ds(src, 16), :]

    mine2 = gath2.at[pl.ds(base2, 256), :]
    gat2 = []
    for t in (2, 1, 3):
        c = remote(mine2, mine2, ag2_s.at[t - 1], ag2_r.at[t - 1], along_b(t))
        c.start()
        gat2.append(c)
    for c in gat2:
        c.wait_recv()

    home = pl.multiple_of(core * 4096, 1024)

    def slab(t, half):
        return g_ref.at[pl.ds(home + mine(t) + half * 512, 512), :]

    def local(half):
        return gath2.at[pl.ds(half * 512, 512), :]

    out = []
    gat1 = {}
    gat1["ra"] = remote(local(0), slab(0, 0), ag1_s.at[0], ag1_r.at[0], right)
    gat1["lb"] = remote(local(1), slab(0, 1), ag1_s.at[1], ag1_r.at[1], left)
    gat1["rb"] = remote(local(1), slab(0, 1), ag1_s.at[2], ag1_r.at[2], right)
    gat1["la"] = remote(local(0), slab(0, 0), ag1_s.at[3], ag1_r.at[3], left)
    for k in ("ra", "lb", "rb", "la"):
        gat1[k].start()
    for h in range(2):
        c = remote(local(h), slab(0, h), out_s.at[h], out_r.at[h], partner)
        c.start()
        out.append(c)
    keep = pltpu.make_async_copy(gath2, g_ref.at[pl.ds(home + mine(0), 1024), :], keep_sem)
    keep.start()
    gat1["ra"].wait_recv()
    fwd_r = remote(slab(3, 0), slab(3, 0), ag1_s.at[4], ag1_r.at[4], right)
    fwd_r.start()
    gat1["lb"].wait_recv()
    fwd_l = remote(slab(1, 1), slab(1, 1), ag1_s.at[5], ag1_r.at[5], left)
    fwd_l.start()

    def hand(n, t, half):
        c = remote(slab(t, half), slab(t, half), out_s.at[n], out_r.at[n], partner)
        c.start()
        out.append(c)

    hand(2, 3, 0)
    hand(3, 1, 1)
    gat1["rb"].wait_recv()
    hand(4, 3, 1)
    gat1["la"].wait_recv()
    hand(5, 1, 0)
    fwd_r.wait_recv()
    hand(6, 2, 0)
    fwd_l.wait_recv()
    hand(7, 2, 1)
    for c in out:
        c.wait_recv()
    keep.wait()
    for c in pairs + [relay_r, relay_l, own_r, own_l, sum_r, sum_l] + sends2 + sends3 + gat3 + gat2:
        c.wait_send()
    for c in list(gat1.values()) + [fwd_r, fwd_l] + out:
        c.wait_send()


def exchange(s, w):
    dma = pltpu.SemaphoreType.DMA
    return pl.pallas_call(
        exchange_kernel,
        out_shape=jax.ShapeDtypeStruct((8192, 128), F32),
        in_specs=[pl.BlockSpec(memory_space=pl.ANY), pl.BlockSpec(memory_space=pltpu.VMEM)],
        out_specs=pl.BlockSpec(memory_space=pl.ANY),
        scratch_shapes=[
            pltpu.VMEM((4096, 128), F32), pltpu.VMEM((4096, 128), F32), pltpu.VMEM((1024, 128), F32),
            pltpu.VMEM((2048, 128), F32), pltpu.VMEM((1024, 128), F32), pltpu.VMEM((768, 128), F32),
            pltpu.VMEM((256, 128), F32), pltpu.VMEM((192, 128), F32), pltpu.VMEM((64, 128), F32),
            pltpu.VMEM((256, 128), F32), pltpu.VMEM((1024, 128), F32),
            dma((4,)), dma((4,)), dma((4,)), dma((6,)), dma((6,)), dma((3,)), dma((3,)), dma((3,)), dma((3,)),
            dma((3,)), dma((3,)), dma((3,)), dma((3,)), dma((6,)), dma((6,)), dma((8,)), dma((8,)), dma(()),
        ],
        compiler_params=pltpu.CompilerParams(collective_id=0, has_side_effects=True, vmem_limit_bytes=24 << 20),
        name="exchange_kernel",
    )(s, w)


def inverse_kernel(
    xa_ref, xb_ref, xc_ref, xd_ref, g_ref, pcol_ref, zrow_ref, lw_ref, bias_ref, o_ref, t_ref,
    u_ref, v_ref, lk_ref, oh_ref, th_ref,
):
    step = pl.program_id(0)

    @pl.when(step == 0)
    def _():
        hi, lo = split(phi_table(pcol_ref))
        v_ref[0:128, :] = hi
        v_ref[128:256, :] = lo
        pick = (iota((128, 16), 0) // 4 % 16 == iota((128, 16), 1)).astype(F32)
        full = lax.Precision.HIGHEST
        rows = lax.dot_general(pick, lw_ref[...], (((1,), (1,)), ((), ())), precision=full, preferred_element_type=F32)
        grid = lax.dot_general(rows, pick, (((1,), (1,)), ((), ())), precision=full, preferred_element_type=F32)
        row, col = iota((128, 128), 0), iota((128, 128), 1)
        same = (row // 64 == col // 64) & (row % 4 == col % 4)
        l_hi, l_lo = split(jnp.where(same, grid, 0.0))
        lk_ref[:, 0:128] = l_hi
        lk_ref[:, 128:256] = l_lo
        zz = lax.axis_index("gz") * ZL + row // 2
        turn = (col % 2 - row % 2) * (Z // 4)
        t_hi, t_lo = split(wave(zz * zrow_ref[...] + turn, Z))
        tt = jnp.concatenate([t_hi, t_lo], axis=1)

        def one(q, carry):
            a = g_ref[pl.ds((q // 16) * 1024 + q % 16, 64, stride=16), :]
            b = g_ref[pl.ds(4096 + q, 64, stride=64), :]
            hi, lo = split(jnp.concatenate([a, b], axis=0))
            top = jnp.concatenate([hi, lo], axis=1)
            low = jnp.concatenate([hi, jnp.zeros_like(lo)], axis=1)
            o = nn(tt, jnp.concatenate([top, low], axis=0))
            u_ref[pl.ds(q, 128, stride=64), :] = o[:, :128] + o[:, 128:]
            return carry

        lax.fori_loop(0, 64, one, 0, unroll=4)

    v_hi, v_lo = v_ref[0:128, :], v_ref[128:256, :]
    l_hi, l_lo = lk_ref[:, 0:128], lk_ref[:, 128:256]
    cat = jnp.concatenate
    for i in range(8):
        u = u_ref[pl.ds(pl.multiple_of((step * 8 + i) * 128, 128), 128), :]
        u_hi, u_lo = split(u.T)
        x_hi, x_lo = split(stack_z((xa_ref, xb_ref, xc_ref, xd_ref), i))
        acc = nn(cat([u_hi, u_lo], axis=1), cat([v_hi, v_hi], axis=0))
        acc = acc + nn(cat([u_hi, l_hi], axis=1), cat([v_lo, x_hi], axis=0))
        acc = acc + nn(cat([l_lo, l_hi], axis=1), cat([x_hi, x_lo], axis=0))
        pre = acc[:64] + bias_ref[...]
        tan = acc[64:]
        sq = pre * pre
        c0 = math.sqrt(2.0 / math.pi)
        t = jnp.tanh(c0 * (pre + 0.044715 * (sq * pre)))
        half = 0.5 * (1.0 + t)
        slope = half + (0.5 * pre) * ((1.0 - t * t) * (c0 * (1.0 + (3.0 * 0.044715) * sq)))
        rows = pl.ds(i, 64, stride=8)
        res, der = pre * half, slope * tan
        for h in range(2):
            oh_ref.at[h][rows, :] = res[:, h * 128 : (h + 1) * 128]
            th_ref.at[h][rows, :] = der[:, h * 128 : (h + 1) * 128]
    for h in range(2):
        o_ref[:, :, h * 128 : (h + 1) * 128] = oh_ref[h].reshape(64, 8, 128)
        t_ref[:, :, h * 128 : (h + 1) * 128] = th_ref[h].reshape(64, 8, 128)


def inverse(field, field_tangent, g, pcol, zrow, lw, bias):
    block = pl.BlockSpec((64, 8, FL), lambda j: (0, j, 0))
    whole = lambda shape: pl.BlockSpec(shape, lambda j: (0,) * len(shape))
    out = jax.ShapeDtypeStruct((64, ZL, FL), F32)
    return pl.pallas_call(
        inverse_kernel,
        grid=(8,),
        out_shape=(out, out),
        in_specs=[
            *halves(), whole((8192, 128)), whole((128, 1)), whole((1, 128)), whole((16, 16)), whole((64, 1)),
        ],
        out_specs=(block, block),
        scratch_shapes=[
            pltpu.VMEM((8192, 128), F32), pltpu.VMEM((256, FL), BF16), pltpu.VMEM((128, 256), BF16),
            pltpu.VMEM((2, 512, 128), F32), pltpu.VMEM((2, 512, 128), F32),
        ],
        compiler_params=pltpu.CompilerParams(vmem_limit_bytes=40 << 20),
        name="inverse_kernel",
    )(field, field, field_tangent, field_tangent, g, pcol, zrow, lw, bias)


def body(field, field_tangent, spectral_weight, local_weight, bias_term, z_modes, phi_modes):
    x0 = field.reshape(64, ZL, FL)
    x1 = field_tangent.reshape(64, ZL, FL)
    zperm = jnp.swapaxes(z_modes.reshape(16, 2, 2), 0, 1).reshape(64)
    zrep = jnp.repeat(zperm, 2)
    prep = jnp.concatenate([phi_modes, phi_modes]).reshape(128, 1)
    w = spectral_weight * SCALE
    c, o, d, lane = (lax.broadcasted_iota(I32, (16, 16, 16, 128), n) for n in range(4))
    lane_o = lane // 4 % 16
    pick = ((o == lane_o) & (c == (lane_o + d) % 16)).astype(F32)
    wd = jnp.einsum("icokq,codl->dikql", w, pick, precision=lax.Precision.HIGHEST).reshape(1024, 128)
    s = forward(x0, x1, prep, zrep.reshape(128, 1))
    g = exchange(s, wd)
    out, tan = inverse(
        x0, x1, g, prep, zrep.reshape(1, 128), local_weight, jnp.repeat(bias_term, 4).reshape(64, 1)
    )
    return out.reshape(16, 4, ZL, FL), tan.reshape(16, 4, ZL, FL)


def solution(mesh):
    return jax.shard_map(
        body,
        mesh=mesh,
        in_specs=(
            P(None, None, "gz", "phi"),
            P(None, None, "gz", "phi"),
            P(None, None, None, "gz", "phi"),
            P(),
            P(),
            P(),
            P(),
        ),
        out_specs=(P(None, None, "gz", "phi"), P(None, None, "gz", "phi")),
        check_vma=False,
    )
```

```python
import functools
import math

import jax
import jax.numpy as jnp
from jax import lax
from jax.experimental import pallas as pl
from jax.experimental.pallas import tpu as pltpu
from jax.sharding import PartitionSpec as P

C, R, ZL, FL = 16, 4, 64, 256
Z, PHI, KZ, KP = 2048, 1024, 64, 64
F32, BF16, I32 = jnp.float32, jnp.bfloat16, jnp.int32
MESH = pl.DeviceIdType.MESH
VMEM_FORWARD = 48 << 20
VMEM_EXCHANGE = 24 << 20
VMEM_INVERSE = 24 << 20
SCALE = (1.0 / math.sqrt(Z * PHI)) * (2.0 / math.sqrt(KZ * KP))


def iota(shape, dim):
    return lax.broadcasted_iota(I32, shape, dim)


def split(x):
    hi = x.astype(BF16)
    return hi, (x - hi.astype(F32)).astype(BF16)


def wave(turns, length):
    quarter = length // 4
    near = ((turns + 2 * quarter) & (length - 1)) - 2 * quarter
    x = (quarter - jnp.abs(near)).astype(F32) * (2.0 * math.pi / length)
    x2 = x * x
    acc = 1.0 / math.factorial(13)
    for n in (11, 9, 7, 5, 3, 1):
        acc = acc * x2 + (1.0 if n % 4 == 1 else -1.0) / math.factorial(n)
    return acc * x


def nt(a, b):
    return lax.dot_general(a, b, (((1,), (1,)), ((), ())), preferred_element_type=F32)


def nn(a, b):
    return jnp.dot(a, b, preferred_element_type=F32)


def pick_column(modes_ref, which):
    hit = iota((128, 64), 1) == which
    return jnp.sum(jnp.where(hit, modes_ref[...].astype(F32), 0.0), axis=1, keepdims=True).astype(I32)


def phi_table(modes_ref):
    row = iota((128, 64), 0)
    col = pick_column(modes_ref, row // 16 * 8 + row % 8)
    f = lax.axis_index("phi") * FL + iota((128, FL), 1)
    return wave(f * col + (iota((128, FL), 0) // 8 % 2) * (PHI // 4), PHI)


def z_table(modes_ref, z, turn):
    row = iota((128, 64), 0)
    col = pick_column(modes_ref, row // 4 % 16 * 4 + row // 64 * 2 + row // 2 % 2)
    return wave((lax.axis_index("gz") * ZL + z) * col + turn, Z)


def places(j):
    q = 2 * j
    base = ((q // 16) * 1024 + (q // 8 % 2) * 128 + q % 8, (q // 8) * 128 + q % 8 + 4096)
    step = (256, 1024)
    return [
        [pl.ds(base[g // 8] + (n + (g % 8 // 2) * step[g // 8] + (g % 2) * 64), 8, stride=8) for g in range(16)]
        for n in range(2)
    ]


def fetch(x0_ref, x1_ref, x_buf, sem, zb):
    copies = []
    for p, src in enumerate((x0_ref, x1_ref)):
        for h in range(2):
            n = zb * 4 + p * 2 + h
            copies.append(pltpu.make_async_copy(
                src.at[:, pl.ds(pl.multiple_of(zb * 8, 8), 8), pl.ds(h * 128, 128)], x_buf.at[n], sem.at[n]
            ))
    return copies


def stack_z(x_buf, zb, i):
    flat = x_buf.reshape(32 * 512, 128)
    a, b, c, d = (flat[pl.ds(zb * 2048 + n * 512 + i, 64, stride=8), :] for n in range(4))
    return jnp.concatenate([jnp.concatenate([a, b], axis=1), jnp.concatenate([c, d], axis=1)], axis=0)


def cat(parts, axis):
    return jnp.concatenate(parts, axis=axis)


def forward_kernel(x0_ref, x1_ref, pm_ref, zm_ref, s_ref, out_ref, x_buf, a_ref, xs_ref, sem, out_sem):
    for zb in range(8):
        for c in fetch(x0_ref, x1_ref, x_buf, sem, zb):
            c.start()
    w_hi, w_lo = split(phi_table(pm_ref))
    w2 = cat([w_hi, w_lo], 0)
    shape = (128, 128)
    turn = (iota(shape, 0) % 2 - iota(shape, 1) // 64) * (Z // 4)
    t_hi, t_lo = split(z_table(zm_ref, iota(shape, 1) % 64, turn))
    t3 = cat([t_hi, t_lo, t_hi], 1)

    def arrive(zb):
        for c in fetch(x0_ref, x1_ref, x_buf, sem, zb):
            c.wait()

    def keep(zb):
        rows = pl.ds(pl.multiple_of(zb * 2048, 2048), 2048)
        return pltpu.make_async_copy(xs_ref.at[rows, :], out_ref.at[rows, :], out_sem.at[zb])

    arrive(0)

    def block(zb, carry):
        @pl.when(zb < 7)
        def _():
            arrive(zb + 1)

        base = pl.multiple_of(zb * 1024, 1024)
        base2 = pl.multiple_of(zb * 2048, 2048)
        for i in range(4):
            for n in range(2):
                hi, lo = split(stack_z(x_buf, zb, i * 2 + n))
                xs_ref[pl.ds(base2 + (i * 512 + n * 128), 128), :] = hi
                xs_ref[pl.ds(base2 + (i * 512 + 256 + n * 128), 128), :] = lo
            hi = xs_ref[pl.ds(base2 + i * 512, 256), :]
            lo = xs_ref[pl.ds(base2 + (i * 512 + 256), 256), :]
            o = nt(w2, hi)
            o = o[:128] + (o[128:] + nt(w_hi, lo))
            for n in range(2):
                a_ref[pl.ds(base + (i * 2 + n), 128, stride=8), :] = o[:, n * 128 : (n + 1) * 128]
        keep(zb).start()
        return carry

    lax.fori_loop(0, 8, block, 0)

    def pair(j, carry):
        base = pl.multiple_of(((j // 4) * 16 + j % 4 * 2) * 8, 16)

        def rows(n):
            return cat([
                a_ref[pl.ds(base + (n * 8 + part * 64 + zb * 1024), 8), :] for part in range(2) for zb in range(8)
            ], 0)

        hi, lo = split(cat([rows(0), rows(1)], 1))
        o = nn(t3, cat([hi, hi, lo], 0))
        spots = places(j)
        for n in range(2):
            for g in range(16):
                s_ref[spots[n][g], :] = o[g * 8 : g * 8 + 8, n * 128 : (n + 1) * 128]
        return carry

    lax.fori_loop(0, 32, pair, 0, unroll=8)
    for zb in range(8):
        keep(zb).wait()


HBM = pl.BlockSpec(memory_space=pltpu.HBM)
VMEM = pl.BlockSpec(memory_space=pltpu.VMEM)


def forward(field, field_tangent, pm, zm):
    packed = jax.ShapeDtypeStruct((16384, FL), BF16)
    return pl.pallas_call(
        forward_kernel,
        out_shape=(jax.ShapeDtypeStruct((8192, 128), F32), packed),
        in_specs=[HBM, HBM, VMEM, VMEM],
        out_specs=(VMEM, HBM),
        scratch_shapes=[
            pltpu.VMEM((32, 64, 8, 128), F32), pltpu.VMEM((8192, 128), F32), pltpu.VMEM((16384, FL), BF16),
            pltpu.SemaphoreType.DMA((32,)), pltpu.SemaphoreType.DMA((8,)),
        ],
        compiler_params=pltpu.CompilerParams(vmem_limit_bytes=VMEM_FORWARD),
        name="forward_kernel",
    )(field, field_tangent, pm, zm)


def mix(x_ref, w_ref, out_ref):
    def pair(ref):
        re = cat([ref[pl.ds(n * 16, 8), :] for n in range(4)], 0)
        im = cat([ref[pl.ds(n * 16 + 8, 8), :] for n in range(4)], 0)
        return re * SCALE, im * SCALE

    xr, xi = pair(x_ref)
    lane = iota((32, 128), 1) % 64
    gr = jnp.zeros((32, 128), F32)
    gi = jnp.zeros((32, 128), F32)
    for d in range(16):
        if d == 0:
            ar, ai = xr, xi
        else:
            near = lane < 64 - 4 * d
            ar = jnp.where(near, pltpu.roll(xr, 128 - 4 * d, 1), pltpu.roll(xr, 64 - 4 * d, 1))
            ai = jnp.where(near, pltpu.roll(xi, 128 - 4 * d, 1), pltpu.roll(xi, 64 - 4 * d, 1))
        wr = w_ref[pl.ds(d * 64, 32), :]
        wi = w_ref[pl.ds(d * 64 + 32, 32), :]
        gr = gr + (ar * wr - ai * wi)
        gi = gi + (ai * wr + ar * wi)
    for n in range(4):
        out_ref[pl.ds(n * 16, 8), :] = gr[n * 8 : n * 8 + 8]
        out_ref[pl.ds(n * 16 + 8, 8), :] = gi[n * 8 : n * 8 + 8]


def exchange_kernel(
    s_ref, w_ref, g_ref,
    peer, acc, relay, fin, second, rec2, third, rec3, own, gath3,
    pair_s, pair_r, st1_s, st1_r, st2_s, st2_r, st3_s, st3_r,
    ag3_s, ag3_r, ag2_s, ag2_r, ag1_s, ag1_r, hand_s, hand_r,
):
    gz = lax.axis_index("gz")
    x = lax.axis_index("phi")
    core = gz % 2
    z = (gz // 2) % 4
    y = gz // 8

    def device(xx, yy, zz, cc):
        return ((yy * 4 + zz) * 2 + cc, xx)

    pa = x + core * (y - x)
    pb = z
    pd = y + core * (x - y)

    def along_a(t):
        n = (pa + t) % 4
        return device(n + core * (x - n), y + core * (n - y), z, core)

    def along_b(t):
        return device(x, y, (z + t) % 4, core)

    def along_d(t):
        n = (pd + t) % 4
        return device(x + core * (n - x), n + core * (y - n), z, core)

    partner = device(x, y, z, 1 - core)

    sent = []

    def send(src, dst, ss, rs, dev):
        c = pltpu.make_async_remote_copy(
            src_ref=src, dst_ref=dst, send_sem=ss, recv_sem=rs, device_id=dev, device_id_type=MESH
        )
        c.start()
        sent.append(c)
        return c

    right, left = along_a(1), along_a(3)
    barrier = pltpu.get_barrier_semaphore()
    peers = [partner, right, left]
    peers += [along_b(t) for t in (1, 2, 3)] + [along_d(t) for t in (1, 2, 3)]
    for dev in peers:
        pl.semaphore_signal(barrier, inc=1, device_id=dev, device_id_type=MESH)
    pl.semaphore_wait(barrier, 9)

    def mine(t):
        return (pa + t) % 4

    qa = y + core * (x - y)
    order = (2, 1, 3, 0)
    pairs = []
    for n, t in enumerate(order):
        pairs.append(send(s_ref.at[1 - core, (qa + t) % 4], peer.at[n], pair_s.at[n], pair_r.at[n], partner))

    def land(n):
        pairs[n].wait_recv()
        acc[n] = s_ref[core, mine(order[n])] + peer[n]

    def piece(slab, s, h, size=4):
        return acc.at[slab, pl.ds(h * 4, size), (pb + s) % 4]

    turns = (2, 1, 3, 0)
    land(0)
    relays = {}
    for s in turns:
        n = s * 6
        relays[0, s] = send(piece(0, s, 0), relay.at[0, s], st1_s.at[n], st1_r.at[n], right)
        relays[1, s] = send(piece(0, s, 1), relay.at[1, s], st1_s.at[n + 1], st1_r.at[n + 1], left)
    land(1)
    land(2)
    first = {}
    for s in turns:
        n = s * 6
        first[s] = [
            send(piece(1, s, 1), fin.at[0, s, pl.ds(4, 4)], st1_s.at[n + 2], st1_r.at[n + 2], right),
            send(piece(2, s, 0), fin.at[1, s, pl.ds(0, 4)], st1_s.at[n + 3], st1_r.at[n + 3], left),
        ]
        for side, dev in enumerate((right, left)):
            relays[side, s].wait_recv()
            ref = piece(1 + side, s, side)
            ref[...] = ref[...] + relay[side, s]
            dst = fin.at[side, s, pl.ds(side * 4, 4)]
            first[s].append(send(ref, dst, st1_s.at[n + 4 + side], st1_r.at[n + 4 + side], dev))
    land(3)

    sends2 = []
    for s in turns:
        for c in first[s]:
            c.wait_recv()
        second[s] = piece(3, s, 0, 8)[...] + (fin[0, s] + fin[1, s])
        if s:
            sends2.append(send(second.at[s], rec2.at[s - 1], st2_s.at[s - 1], st2_r.at[s - 1], along_b(s)))
    for c in sends2:
        c.wait_recv()
    third[...] = (second[0] + rec2[0] + (rec2[1] + rec2[2])).reshape(4, 64, 128)

    sends3 = []
    for t in turns[:3]:
        sends3.append(send(third.at[(pd + t) % 4], rec3.at[t - 1], st3_s.at[t - 1], st3_r.at[t - 1], along_d(t)))
    for c in sends3:
        c.wait_recv()
    own[...] = third[pd] + rec3[0] + (rec3[1] + rec3[2])
    mine3 = gath3.at[pd]
    mix(own, w_ref, mine3)

    gat3 = [send(mine3, mine3, ag3_s.at[t - 1], ag3_r.at[t - 1], along_d(t)) for t in turns[:3]]
    for c in gat3:
        c.wait_recv()

    def spot(t, s, h, size=4):
        return g_ref.at[core, mine(t), pl.ds(h * 4, size), (pb + s) % 4]

    mine2 = spot(0, 0, 0, 8)
    mine2[...] = gath3[...].reshape(8, 32, 128)

    gat2 = {t: send(mine2, mine2, ag2_s.at[t - 1], ag2_r.at[t - 1], along_b(t)) for t in (1, 3, 2)}
    gat1 = {}
    hands = []

    def pass_on(u, key, t, h, dev):
        n = u * 6 + ("ra", "lb", "rb", "la", "fr", "fl").index(key)
        gat1[u, key] = send(spot(t, u, h), spot(t, u, h), ag1_s.at[n], ag1_r.at[n], dev)

    def hand(u, n, t, h, size=4):
        ref = spot(t, u, h, size)
        hands.append(send(ref, ref, hand_s.at[u * 7 + n], hand_r.at[u * 7 + n], partner))

    def emit(u):
        pass_on(u, "ra", 0, 0, right)
        pass_on(u, "lb", 0, 1, left)
        pass_on(u, "rb", 0, 1, right)
        pass_on(u, "la", 0, 0, left)
        hand(u, 0, 0, 0, 8)

    def turn_round(u):
        gat1[u, "ra"].wait_recv()
        pass_on(u, "fr", 3, 0, right)
        gat1[u, "lb"].wait_recv()
        pass_on(u, "fl", 1, 1, left)
        hand(u, 1, 3, 0)
        hand(u, 2, 1, 1)

    emit(0)
    gat2[1].wait_recv()
    emit(3)
    turn_round(0)
    gat2[3].wait_recv()
    emit(1)
    turn_round(3)
    gat2[2].wait_recv()
    emit(2)
    turn_round(1)
    turn_round(2)
    for u in (0, 3, 1, 2):
        gat1[u, "rb"].wait_recv()
        hand(u, 3, 3, 1)
        gat1[u, "la"].wait_recv()
        hand(u, 4, 1, 0)
        gat1[u, "fr"].wait_recv()
        hand(u, 5, 2, 0)
        gat1[u, "fl"].wait_recv()
        hand(u, 6, 2, 1)
    for c in hands:
        c.wait_recv()
    for c in sent:
        c.wait_send()


def exchange(s, w):
    dma = pltpu.SemaphoreType.DMA
    buf = lambda *dims: pltpu.VMEM((*dims, 128), F32)
    return pl.pallas_call(
        exchange_kernel,
        out_shape=jax.ShapeDtypeStruct((2, 4, 8, 4, 32, 128), F32),
        in_specs=[VMEM, VMEM],
        out_specs=VMEM,
        scratch_shapes=[
            buf(4, 8, 4, 32), buf(4, 8, 4, 32), buf(2, 4, 4, 32), buf(2, 4, 8, 32), buf(4, 8, 32), buf(3, 8, 32),
            buf(4, 64), buf(3, 64), buf(64), buf(4, 64),
            dma((4,)), dma((4,)), dma((24,)), dma((24,)), dma((3,)), dma((3,)), dma((3,)), dma((3,)),
            dma((3,)), dma((3,)), dma((3,)), dma((3,)), dma((24,)), dma((24,)), dma((28,)), dma((28,)),
        ],
        compiler_params=pltpu.CompilerParams(collective_id=0, has_side_effects=True, vmem_limit_bytes=VMEM_EXCHANGE),
        name="exchange_kernel",
    )(s.reshape(2, 4, 8, 4, 32, 128), w).reshape(8192, 128)


def inverse_kernel(
    xs_ref, g_ref, pm_ref, zm_ref, lw_ref, bias_ref, o_ref, t_ref, u_ref, acc_ref, out_buf, out_sem
):
    shape = (128, 128)
    row, col = iota(shape, 0), iota(shape, 1)
    turn = (row % 2 - col % 2) * (Z // 4)
    t_hi, t_lo = split(z_table(zm_ref, col // 2, turn).T)
    t3 = cat([t_hi, t_lo, t_hi], 1)

    def pair(j, carry):
        spots = places(j)
        g2 = cat([cat([g_ref[spots[n][g], :] for g in range(16)], 0) for n in range(2)], 1)
        hi, lo = split(g2)
        o = nn(t3, cat([hi, hi, lo], 0))
        base = (j // 4) * 1024 + j % 4 * 2
        for n in range(2):
            for g in range(16):
                u_ref[pl.ds(base + (n + g * 64), 8, stride=8), :] = o[g * 8 : g * 8 + 8, n * 128 : (n + 1) * 128]
        return carry

    lax.fori_loop(0, 32, pair, 0, unroll=8)
    v_hi, v_lo = split(phi_table(pm_ref))
    pick = (iota((128, 16), 0) // 4 % 16 == iota((128, 16), 1)).astype(F32)
    full = lax.Precision.HIGHEST
    rows = lax.dot_general(pick, lw_ref[...], (((1,), (1,)), ((), ())), precision=full, preferred_element_type=F32)
    grid = lax.dot_general(rows, pick, (((1,), (1,)), ((), ())), precision=full, preferred_element_type=F32)
    same = (row // 64 == col // 64) & (row % 4 == col % 4)
    l_hi, l_lo = split(jnp.where(same, grid, 0.0))
    bias = jnp.sum(jnp.where(iota((64, 16), 0) // 4 == iota((64, 16), 1), bias_ref[...], 0.0), axis=1, keepdims=True)
    c0 = math.sqrt(2.0 / math.pi)

    def copies(zb, slot):
        out = []
        for n, dst in enumerate((o_ref, t_ref)):
            for h in range(2):
                out.append(pltpu.make_async_copy(
                    out_buf.at[slot * 4 + n * 2 + h], dst.at[:, pl.ds(pl.multiple_of(zb * 8, 8), 8), pl.ds(h * 128, 128)],
                    out_sem.at[slot * 4 + n * 2 + h],
                ))
        return out

    def gather_z(z, slot):
        z16 = z * 16
        u = cat([u_ref[pl.ds(pl.multiple_of(n * 1024 + z16, 16), 16), :] for n in range(8)], 0)
        u_hi, u_lo = split(u.T)
        zrow = (z // 2) * 512 + (z % 2) * 128
        hi = xs_ref[pl.ds(pl.multiple_of(zrow, 128), 128), :]
        lo = xs_ref[pl.ds(pl.multiple_of(zrow + 256, 128), 128), :]
        acc_ref[slot] = nn(cat([u_hi, u_lo, u_hi, l_hi, l_lo, l_hi], 1), cat([v_hi, v_hi, v_lo, hi, hi, lo], 0))

    gather_z(0, 0)

    def block(zb, carry):
        slot = zb % 2

        @pl.when(zb >= 2)
        def _():
            for c in copies(zb, slot):
                c.wait()

        flat = out_buf.reshape(8 * 512, 128)
        for i in range(8):
            gather_z(jnp.minimum(zb * 8 + i + 1, 63), (i + 1) % 2)
            pre = acc_ref[i % 2, 0:64, :] + bias
            tan = acc_ref[i % 2, 64:128, :]
            sq = pre * pre
            t = jnp.tanh(pre * (c0 + (c0 * 0.044715) * sq))
            half = 0.5 + 0.5 * t
            slope = half + (0.5 * pre) * ((1.0 - t * t) * (c0 + (3.0 * 0.044715 * c0) * sq))
            for n, val in enumerate((pre * half, slope * tan)):
                for h in range(2):
                    flat[pl.ds(slot * 2048 + n * 1024 + h * 512 + i, 64, stride=8), :] = val[:, h * 128 : (h + 1) * 128]
        for c in copies(zb, slot):
            c.start()
        return carry

    lax.fori_loop(0, 8, block, 0)
    for zb in (6, 7):
        for c in copies(zb, zb % 2):
            c.wait()


def inverse(xs, g, pm, zm, lw, bias):
    out = jax.ShapeDtypeStruct((64, ZL, FL), F32)
    return pl.pallas_call(
        inverse_kernel,
        out_shape=(out, out),
        in_specs=[VMEM, VMEM, VMEM, VMEM, VMEM, VMEM],
        out_specs=(HBM, HBM),
        scratch_shapes=[
            pltpu.VMEM((8192, 128), F32), pltpu.VMEM((2, 128, FL), F32), pltpu.VMEM((8, 64, 8, 128), F32),
            pltpu.SemaphoreType.DMA((8,)),
        ],
        compiler_params=pltpu.CompilerParams(vmem_limit_bytes=VMEM_INVERSE),
        name="inverse_kernel",
    )(xs, g, pm, zm, lw, bias)


def body(field, field_tangent, spectral_weight, local_weight, bias_term, z_modes, phi_modes):
    x0 = field.reshape(64, ZL, FL)
    x1 = field_tangent.reshape(64, ZL, FL)
    zm = z_modes.reshape(1, 64)
    pm = phi_modes.reshape(1, 64)
    w = spectral_weight.reshape(2, 16, 16, 2, 2, 8)
    c, o, d, lane = (lax.broadcasted_iota(I32, (16, 16, 16, 128), n) for n in range(4))
    lane_o = lane // 4 % 16
    pick = ((o == lane_o) & (c == (lane_o + d) % 16)).astype(F32)
    wd = jnp.einsum("icokhq,codl->dihkql", w, pick, precision=lax.Precision.HIGHEST).reshape(1024, 128)
    s, xs = forward(x0, x1, pm, zm)
    g = exchange(s, wd)
    out, tan = inverse(xs, g, pm, zm, local_weight, bias_term.reshape(1, 16))
    return out.reshape(16, 4, ZL, FL), tan.reshape(16, 4, ZL, FL)


def solution(mesh):
    return jax.shard_map(
        body,
        mesh=mesh,
        in_specs=(
            P(None, None, "gz", "phi"),
            P(None, None, "gz", "phi"),
            P(None, None, None, "gz", "phi"),
            P(),
            P(),
            P(),
            P(),
        ),
        out_specs=(P(None, None, "gz", "phi"), P(None, None, "gz", "phi")),
        check_vma=False,
    )
```

```python
import functools
import math

import jax
import jax.numpy as jnp
from jax import lax
from jax.experimental import pallas as pl
from jax.experimental.pallas import tpu as pltpu
from jax.sharding import PartitionSpec as P

C, R, ZL, FL = 16, 4, 64, 256
Z, PHI, KZ, KP = 2048, 1024, 64, 64
F32, BF16, I32 = jnp.float32, jnp.bfloat16, jnp.int32
MESH = pl.DeviceIdType.MESH
VMEM_EXCHANGE = 46 << 20
VMEM_INVERSE = 44 << 20
SCALE = (1.0 / math.sqrt(Z * PHI)) * (2.0 / math.sqrt(KZ * KP))


def iota(shape, dim):
    return lax.broadcasted_iota(I32, shape, dim)


def split(x):
    hi = x.astype(BF16)
    return hi, (x - hi.astype(F32)).astype(BF16)


def wave(turns, length):
    quarter = length // 4
    near = ((turns + 2 * quarter) & (length - 1)) - 2 * quarter
    x = (quarter - jnp.abs(near)).astype(F32) * (2.0 * math.pi / length)
    x2 = x * x
    acc = 1.0 / math.factorial(13)
    for n in (11, 9, 7, 5, 3, 1):
        acc = acc * x2 + (1.0 if n % 4 == 1 else -1.0) / math.factorial(n)
    return acc * x


def nt(a, b):
    return lax.dot_general(a, b, (((1,), (1,)), ((), ())), preferred_element_type=F32)


def nn(a, b):
    return jnp.dot(a, b, preferred_element_type=F32)


def pick_column(modes_ref, which):
    hit = iota((128, 64), 1) == which
    return jnp.sum(jnp.where(hit, modes_ref[...].astype(F32), 0.0), axis=1, keepdims=True).astype(I32)


def phi_table(modes_ref):
    row = iota((128, 64), 0)
    col = pick_column(modes_ref, row // 16 * 8 + row % 8)
    f = lax.axis_index("phi") * FL + iota((128, FL), 1)
    return wave(f * col + (iota((128, FL), 0) // 8 % 2) * (PHI // 4), PHI)


def z_table(modes_ref, z, turn):
    row = iota((128, 64), 0)
    col = pick_column(modes_ref, row // 4 % 16 * 4 + row // 64 * 2 + row // 2 % 2)
    return wave((lax.axis_index("gz") * ZL + z) * col + turn, Z)


def places(j):
    q = 2 * j
    base = ((q // 16) * 1024 + (q // 8 % 2) * 128 + q % 8, (q // 8) * 128 + q % 8 + 4096)
    step = (256, 1024)
    return [
        [pl.ds(base[g // 8] + (n + (g % 8 // 2) * step[g // 8] + (g % 2) * 64), 8, stride=8) for g in range(16)]
        for n in range(2)
    ]


def fetch(x0_ref, x1_ref, x_buf, sem, zb):
    copies = []
    for p, src in enumerate((x0_ref, x1_ref)):
        for h in range(2):
            n = zb * 4 + p * 2 + h
            copies.append(pltpu.make_async_copy(
                src.at[:, pl.ds(pl.multiple_of(zb * 8, 8), 8), pl.ds(h * 128, 128)], x_buf.at[n], sem.at[n]
            ))
    return copies


def stack_z(x_buf, zb, i):
    flat = x_buf.reshape(32 * 512, 128)
    a, b, c, d = (flat[pl.ds(zb * 2048 + n * 512 + i, 64, stride=8), :] for n in range(4))
    return jnp.concatenate([jnp.concatenate([a, b], axis=1), jnp.concatenate([c, d], axis=1)], axis=0)


def cat(parts, axis):
    return jnp.concatenate(parts, axis=axis)


def transform(x0_ref, x1_ref, pm_ref, zm_ref, s_ref, x_buf, a_ref, xs_ref, v_ref, sem):
    for zb in range(8):
        for c in fetch(x0_ref, x1_ref, x_buf, sem, zb):
            c.start()
    w_hi, w_lo = split(phi_table(pm_ref))
    w2 = cat([w_hi, w_lo], 0)
    v_ref[...] = w2
    shape = (128, 128)
    turn = (iota(shape, 0) % 2 - iota(shape, 1) // 64) * (Z // 4)
    t_hi, t_lo = split(z_table(zm_ref, iota(shape, 1) % 64, turn))
    t3 = cat([t_hi, t_lo, t_hi], 1)

    def arrive(zb):
        for c in fetch(x0_ref, x1_ref, x_buf, sem, zb):
            c.wait()

    arrive(0)

    def block(zb, carry):
        @pl.when(zb < 7)
        def _():
            arrive(zb + 1)

        base = pl.multiple_of(zb * 1024, 1024)
        base2 = pl.multiple_of(zb * 2048, 2048)
        for i in range(4):
            for n in range(2):
                hi, lo = split(stack_z(x_buf, zb, i * 2 + n))
                xs_ref[pl.ds(base2 + (i * 512 + n * 128), 128), :] = hi
                xs_ref[pl.ds(base2 + (i * 512 + 256 + n * 128), 128), :] = lo
            hi = xs_ref[pl.ds(base2 + i * 512, 256), :]
            lo = xs_ref[pl.ds(base2 + (i * 512 + 256), 256), :]
            o = nt(w2, hi)
            o = o[:128] + (o[128:] + nt(w_hi, lo))
            for n in range(2):
                a_ref[pl.ds(base + (i * 2 + n), 128, stride=8), :] = o[:, n * 128 : (n + 1) * 128]
        return carry

    lax.fori_loop(0, 8, block, 0)

    def pair(j, carry):
        base = pl.multiple_of(((j // 4) * 16 + j % 4 * 2) * 8, 16)

        def rows(n):
            return cat([
                a_ref[pl.ds(base + (n * 8 + part * 64 + zb * 1024), 8), :] for part in range(2) for zb in range(8)
            ], 0)

        hi, lo = split(cat([rows(0), rows(1)], 1))
        o = nn(t3, cat([hi, hi, lo], 0))
        spots = places(j)
        for n in range(2):
            for g in range(16):
                s_ref[spots[n][g], :] = o[g * 8 : g * 8 + 8, n * 128 : (n + 1) * 128]
        return carry

    lax.fori_loop(0, 32, pair, 0, unroll=8)


def inverse_z(modes_ref, t_ref):
    row, col = iota((128, 128), 0), iota((128, 128), 1)
    turn = (row % 2 - col % 2) * (Z // 4)
    hi, lo = split(z_table(modes_ref, col // 2, turn).T)
    t_ref[:, 0:128] = hi
    t_ref[:, 128:256] = lo


def local_mixing(lw_ref, bias_ref):
    pick = (iota((128, 16), 0) // 4 % 16 == iota((128, 16), 1)).astype(F32)
    full = lax.Precision.HIGHEST
    rows = lax.dot_general(pick, lw_ref[...], (((1,), (1,)), ((), ())), precision=full, preferred_element_type=F32)
    grid = lax.dot_general(rows, pick, (((1,), (1,)), ((), ())), precision=full, preferred_element_type=F32)
    row, col = iota((128, 128), 0), iota((128, 128), 1)
    same = (row // 64 == col // 64) & (row % 4 == col % 4)
    l_hi, l_lo = split(jnp.where(same, grid, 0.0))
    here = (iota((128, 16), 0) // 4 == iota((128, 16), 1))
    bias = jnp.sum(jnp.where(here, bias_ref[...], 0.0), axis=1, keepdims=True)
    return cat([l_hi, l_lo, l_hi], 1), bias


HBM = pl.BlockSpec(memory_space=pltpu.HBM)
VMEM = pl.BlockSpec(memory_space=pltpu.VMEM)


def mix(x_ref, w_ref, out_ref):
    def pair(ref):
        re = cat([ref[pl.ds(n * 16, 8), :] for n in range(4)], 0)
        im = cat([ref[pl.ds(n * 16 + 8, 8), :] for n in range(4)], 0)
        return re * SCALE, im * SCALE

    xr, xi = pair(x_ref)
    lane = iota((32, 128), 1) % 64
    gr = jnp.zeros((32, 128), F32)
    gi = jnp.zeros((32, 128), F32)
    for d in range(16):
        if d == 0:
            ar, ai = xr, xi
        else:
            near = lane < 64 - 4 * d
            ar = jnp.where(near, pltpu.roll(xr, 128 - 4 * d, 1), pltpu.roll(xr, 64 - 4 * d, 1))
            ai = jnp.where(near, pltpu.roll(xi, 128 - 4 * d, 1), pltpu.roll(xi, 64 - 4 * d, 1))
        wr = w_ref[pl.ds(d * 64, 32), :]
        wi = w_ref[pl.ds(d * 64 + 32, 32), :]
        gr = gr + (ar * wr - ai * wi)
        gi = gi + (ai * wr + ar * wi)
    for n in range(4):
        out_ref[pl.ds(n * 16, 8), :] = gr[n * 8 : n * 8 + 8]
        out_ref[pl.ds(n * 16 + 8, 8), :] = gi[n * 8 : n * 8 + 8]


def exchange_kernel(
    x0_ref, x1_ref, pm_ref, zm_ref, w_ref, lw_ref, bias_ref, g_ref, loc_ref, v_ref, t_ref,
    x_buf, a_ref, xs_ref, spec_ref, loc_buf, x_sem, loc_sem, peer, acc, relay, fin, second, relay2, rec2, third, rec3, own, gath3,
    pair_s, pair_r, st1_s, st1_r, st2_s, st2_r, st3_s, st3_r,
    ag3_s, ag3_r, ag2_s, ag2_r, ag1_s, ag1_r, hand_s, hand_r,
):
    gz = lax.axis_index("gz")
    x = lax.axis_index("phi")
    core = gz % 2
    z = (gz // 2) % 4
    y = gz // 8

    def device(xx, yy, zz, cc):
        return ((yy * 4 + zz) * 2 + cc, xx)

    pa = x + core * (y - x)
    pb = z
    pd = y + core * (x - y)

    def along_a(t):
        n = (pa + t) % 4
        return device(n + core * (x - n), y + core * (n - y), z, core)

    def along_b(t):
        return device(x, y, (z + t) % 4, core)

    def along_d(t):
        n = (pd + t) % 4
        return device(x + core * (n - x), n + core * (y - n), z, core)

    partner = device(x, y, z, 1 - core)

    sent = []

    def send(src, dst, ss, rs, dev):
        c = pltpu.make_async_remote_copy(
            src_ref=src, dst_ref=dst, send_sem=ss, recv_sem=rs, device_id=dev, device_id_type=MESH
        )
        c.start()
        sent.append(c)
        return c

    right, left = along_a(1), along_a(3)
    barrier = pltpu.get_barrier_semaphore()
    peers = [partner, right, left]
    peers += [along_b(1), along_b(3)] + [along_d(t) for t in (1, 2, 3)]
    for dev in peers:
        pl.semaphore_signal(barrier, inc=1, device_id=dev, device_id_type=MESH)
    transform(x0_ref, x1_ref, pm_ref, zm_ref, spec_ref, x_buf, a_ref, xs_ref, v_ref, x_sem)
    s_ref = spec_ref.reshape(2, 4, 8, 4, 32, 128)
    pl.semaphore_wait(barrier, 8)

    def mine(t):
        return (pa + t) % 4

    qa = y + core * (x - y)
    order = (2, 1, 3, 0)
    pairs = []
    for n, t in enumerate(order):
        pairs.append(send(s_ref.at[1 - core, (qa + t) % 4], peer.at[n], pair_s.at[n], pair_r.at[n], partner))

    l3, bias = local_mixing(lw_ref, bias_ref)
    stores = []

    def mix_local(zb):
        slot = zb % 2
        if zb >= 2:
            stores[zb - 2].wait()

        def four(i, carry):
            for n in range(4):
                row = (zb * 4 + n // 2) * 512 + n % 2 * 128
                hi = xs_ref[pl.ds(pl.multiple_of(i * 1024 + row, 128), 128), :]
                lo = xs_ref[pl.ds(pl.multiple_of(i * 1024 + row + 256, 128), 128), :]
                o = nn(l3, cat([hi, hi, lo], 0)) + bias
                loc_buf[slot, pl.ds(pl.multiple_of(i * 512 + n * 128, 128), 128), :] = o
            return carry

        lax.fori_loop(0, 2, four, 0)
        c = pltpu.make_async_copy(loc_buf.at[slot], loc_ref.at[pl.ds(zb * 1024, 1024), :], loc_sem.at[zb])
        c.start()
        stores.append(c)

    mix_local(0)
    mix_local(1)

    def land(n):
        pairs[n].wait_recv()
        acc[n] = s_ref[core, mine(order[n])] + peer[n]

    def piece(slab, s, h, size=4):
        return acc.at[slab, pl.ds(h * 4, size), (pb + s) % 4]

    turns = (2, 1, 3, 0)
    land(0)
    relays = {}
    for s in turns:
        n = s * 6
        relays[0, s] = send(piece(0, s, 0), relay.at[0, s], st1_s.at[n], st1_r.at[n], right)
        relays[1, s] = send(piece(0, s, 1), relay.at[1, s], st1_s.at[n + 1], st1_r.at[n + 1], left)
    mix_local(2)
    land(1)
    land(2)
    first = {}
    for s in turns:
        n = s * 6
        first[s] = [
            send(piece(1, s, 1), fin.at[0, s, pl.ds(4, 4)], st1_s.at[n + 2], st1_r.at[n + 2], right),
            send(piece(2, s, 0), fin.at[1, s, pl.ds(0, 4)], st1_s.at[n + 3], st1_r.at[n + 3], left),
        ]
        mix_local(3 + turns.index(s))
        for side, dev in enumerate((right, left)):
            relays[side, s].wait_recv()
            ref = piece(1 + side, s, side)
            ref[...] = ref[...] + relay[side, s]
            dst = fin.at[side, s, pl.ds(side * 4, 4)]
            first[s].append(send(ref, dst, st1_s.at[n + 4 + side], st1_r.at[n + 4 + side], dev))
    land(3)

    sends2 = []
    for s in turns:
        for c in first[s]:
            c.wait_recv()
        second[s] = piece(3, s, 0, 8)[...] + (fin[0, s] + fin[1, s])
        if s == 2:
            far = [
                send(second.at[2, pl.ds(h * 4, 4)], relay2.at[h], st2_s.at[h], st2_r.at[h], along_b(1 + 2 * h))
                for h in range(2)
            ]
        elif s:
            h = s // 2
            far[h].wait_recv()
            part = second.at[s, pl.ds(h * 4, 4)]
            part[...] = part[...] + relay2[h]
            sends2.append(send(second.at[s], rec2.at[h], st2_s.at[2 + h], st2_r.at[2 + h], along_b(s)))
    mix_local(7)
    for c in sends2:
        c.wait_recv()
    third[...] = (second[0] + (rec2[0] + rec2[1])).reshape(4, 64, 128)

    sends3 = []
    for t in turns[:3]:
        sends3.append(send(third.at[(pd + t) % 4], rec3.at[t - 1], st3_s.at[t - 1], st3_r.at[t - 1], along_d(t)))
    for c in sends3:
        c.wait_recv()
    own[...] = third[pd] + rec3[0] + (rec3[1] + rec3[2])
    mine3 = gath3.at[pd]
    mix(own, w_ref, mine3)

    gat3 = [send(mine3, mine3, ag3_s.at[t - 1], ag3_r.at[t - 1], along_d(t)) for t in turns[:3]]
    inverse_z(zm_ref, t_ref)
    for c in gat3:
        c.wait_recv()

    def spot(t, s, h, size=4):
        return g_ref.at[core, mine(t), pl.ds(h * 4, size), (pb + s) % 4]

    mine2 = spot(0, 0, 0, 8)
    mine2[...] = gath3[...].reshape(8, 32, 128)

    gat2, gat1, hands = {}, {}, []

    def pass_b(key, u, h, t):
        n = ("ra", "lb", "rb", "la", "fr", "fl").index(key)
        gat2[key] = send(spot(0, u, h), spot(0, u, h), ag2_s.at[n], ag2_r.at[n], along_b(t))

    def pass_a(key, u, t, h, dev):
        n = u * 6 + ("ra", "lb", "rb", "la", "fr", "fl").index(key)
        gat1[u, key] = send(spot(t, u, h), spot(t, u, h), ag1_s.at[n], ag1_r.at[n], dev)

    def hand(u, n, t, h):
        ref = spot(t, u, h)
        hands.append(send(ref, ref, hand_s.at[u * 8 + n], hand_r.at[u * 8 + n], partner))

    def emit(u, h):
        if h == 0:
            pass_a("ra", u, 0, 0, right)
            pass_a("la", u, 0, 0, left)
        else:
            pass_a("lb", u, 0, 1, left)
            pass_a("rb", u, 0, 1, right)
        hand(u, h, 0, h)

    def turn_round(u):
        gat1[u, "ra"].wait_recv()
        pass_a("fr", u, 3, 0, right)
        gat1[u, "lb"].wait_recv()
        pass_a("fl", u, 1, 1, left)
        hand(u, 2, 3, 0)
        hand(u, 3, 1, 1)

    pass_b("ra", 0, 0, 1)
    pass_b("lb", 0, 1, 3)
    pass_b("rb", 0, 1, 1)
    pass_b("la", 0, 0, 3)
    emit(0, 0)
    emit(0, 1)
    gat2["ra"].wait_recv()
    pass_b("fr", 3, 0, 1)
    gat2["lb"].wait_recv()
    pass_b("fl", 1, 1, 3)
    emit(3, 0)
    emit(1, 1)
    turn_round(0)
    gat2["rb"].wait_recv()
    emit(3, 1)
    gat2["la"].wait_recv()
    emit(1, 0)
    gat2["fr"].wait_recv()
    emit(2, 0)
    gat2["fl"].wait_recv()
    emit(2, 1)
    for u in (3, 1, 2):
        turn_round(u)
    for u in (0, 3, 1, 2):
        gat1[u, "rb"].wait_recv()
        hand(u, 4, 3, 1)
        gat1[u, "la"].wait_recv()
        hand(u, 5, 1, 0)
        gat1[u, "fr"].wait_recv()
        hand(u, 6, 2, 0)
        gat1[u, "fl"].wait_recv()
        hand(u, 7, 2, 1)
    for c in hands:
        c.wait_recv()
    for c in sent:
        c.wait_send()
    for c in stores[6:]:
        c.wait()


def exchange(field, field_tangent, pm, zm, wt, lw, bias):
    dma = pltpu.SemaphoreType.DMA
    buf = lambda *dims: pltpu.VMEM((*dims, 128), F32)
    table = jax.ShapeDtypeStruct((256, 256), BF16)
    return pl.pallas_call(
        exchange_kernel,
        out_shape=(
            jax.ShapeDtypeStruct((2, 4, 8, 4, 32, 128), F32), jax.ShapeDtypeStruct((8192, FL), F32),
            table, jax.ShapeDtypeStruct((128, 256), BF16),
        ),
        in_specs=[HBM, HBM, VMEM, VMEM, VMEM, VMEM, VMEM],
        out_specs=(VMEM, HBM, VMEM, VMEM),
        scratch_shapes=[
            buf(32, 64, 8), buf(8192), pltpu.VMEM((16384, FL), BF16), buf(8192),
            pltpu.VMEM((2, 1024, FL), F32), dma((32,)), dma((8,)),
            buf(4, 8, 4, 32), buf(4, 8, 4, 32), buf(2, 4, 4, 32), buf(2, 4, 8, 32), buf(4, 8, 32), buf(2, 4, 32), buf(2, 8, 32),
            buf(4, 64), buf(3, 64), buf(64), buf(4, 64),
            dma((4,)), dma((4,)), dma((24,)), dma((24,)), dma((4,)), dma((4,)), dma((3,)), dma((3,)),
            dma((3,)), dma((3,)), dma((6,)), dma((6,)), dma((24,)), dma((24,)), dma((32,)), dma((32,)),
        ],
        compiler_params=pltpu.CompilerParams(collective_id=0, has_side_effects=True, vmem_limit_bytes=VMEM_EXCHANGE),
        name="exchange_kernel",
    )(field, field_tangent, pm, zm, wt, lw, bias)


def inverse_kernel(
    loc_hbm, g_ref, v_ref, tz_ref, o_ref, t_ref, loc_ref, u_ref, acc_ref, out_buf, loc_sem, out_sem
):
    def take(zb):
        rows = pl.ds(pl.multiple_of(zb * 1024, 1024), 1024)
        return pltpu.make_async_copy(loc_hbm.at[rows, :], loc_ref.at[rows, :], loc_sem.at[zb])

    for zb in range(8):
        take(zb).start()
    t_hi, t_lo = tz_ref[:, 0:128], tz_ref[:, 128:256]
    t3 = cat([t_hi, t_lo, t_hi], 1)

    def pair(j, carry):
        spots = places(j)
        g2 = cat([cat([g_ref[spots[n][g], :] for g in range(16)], 0) for n in range(2)], 1)
        hi, lo = split(g2)
        o = nn(t3, cat([hi, hi, lo], 0))
        base = (j // 4) * 1024 + j % 4 * 2
        for n in range(2):
            for g in range(16):
                u_ref[pl.ds(base + (n + g * 64), 8, stride=8), :] = o[g * 8 : g * 8 + 8, n * 128 : (n + 1) * 128]
        return carry

    lax.fori_loop(0, 32, pair, 0, unroll=8)
    v_hi, v_lo = v_ref[0:128, :], v_ref[128:256, :]
    v3 = cat([v_hi, v_hi, v_lo], 0)
    c0 = math.sqrt(2.0 / math.pi)

    def copies(zb, slot):
        out = []
        for n, dst in enumerate((o_ref, t_ref)):
            for h in range(2):
                out.append(pltpu.make_async_copy(
                    out_buf.at[slot * 4 + n * 2 + h], dst.at[:, pl.ds(pl.multiple_of(zb * 8, 8), 8), pl.ds(h * 128, 128)],
                    out_sem.at[slot * 4 + n * 2 + h],
                ))
        return out

    def gather_z(z, slot):
        z16 = z * 16
        u = cat([u_ref[pl.ds(pl.multiple_of(n * 1024 + z16, 16), 16), :] for n in range(8)], 0)
        u_hi, u_lo = split(u.T)
        local = loc_ref[pl.ds(pl.multiple_of(z * 128, 128), 128), :]
        acc_ref[slot] = nn(cat([u_hi, u_lo, u_hi], 1), v3) + local

    take(0).wait()
    gather_z(0, 0)

    def block(zb, carry):
        slot = zb % 2

        @pl.when(zb < 7)
        def _():
            take(zb + 1).wait()

        @pl.when(zb >= 2)
        def _():
            for c in copies(zb, slot):
                c.wait()

        flat = out_buf.reshape(8 * 512, 128)
        for i in range(8):
            gather_z(jnp.minimum(zb * 8 + i + 1, 63), (i + 1) % 2)
            pre = acc_ref[i % 2, 0:64, :]
            tan = acc_ref[i % 2, 64:128, :]
            sq = pre * pre
            t = jnp.tanh(pre * (c0 + (c0 * 0.044715) * sq))
            half = 0.5 + 0.5 * t
            res = pre * half
            slope = half + res * ((1.0 - t) * (c0 + (3.0 * 0.044715 * c0) * sq))
            for n, val in enumerate((res, slope * tan)):
                for h in range(2):
                    flat[pl.ds(slot * 2048 + n * 1024 + h * 512 + i, 64, stride=8), :] = val[:, h * 128 : (h + 1) * 128]
        for c in copies(zb, slot):
            c.start()
        return carry

    lax.fori_loop(0, 8, block, 0)
    for zb in (6, 7):
        for c in copies(zb, zb % 2):
            c.wait()


def inverse(loc, g, v, tz):
    out = jax.ShapeDtypeStruct((64, ZL, FL), F32)
    return pl.pallas_call(
        inverse_kernel,
        out_shape=(out, out),
        in_specs=[HBM, VMEM, VMEM, VMEM],
        out_specs=(HBM, HBM),
        scratch_shapes=[
            pltpu.VMEM((8192, FL), F32), pltpu.VMEM((8192, 128), F32), pltpu.VMEM((2, 128, FL), F32), pltpu.VMEM((8, 64, 8, 128), F32),
            pltpu.SemaphoreType.DMA((8,)), pltpu.SemaphoreType.DMA((8,)),
        ],
        compiler_params=pltpu.CompilerParams(vmem_limit_bytes=VMEM_INVERSE),
        name="inverse_kernel",
    )(loc, g, v, tz)


def body(field, field_tangent, spectral_weight, local_weight, bias_term, z_modes, phi_modes):
    x0 = field.reshape(64, ZL, FL)
    x1 = field_tangent.reshape(64, ZL, FL)
    zm = z_modes.reshape(1, 64)
    pm = phi_modes.reshape(1, 64)
    w = spectral_weight.reshape(2, 16, 16, 2, 2, 8)
    c, o, d, lane = (lax.broadcasted_iota(I32, (16, 16, 16, 128), n) for n in range(4))
    lane_o = lane // 4 % 16
    pick = ((o == lane_o) & (c == (lane_o + d) % 16)).astype(F32)
    wd = jnp.einsum("icokhq,codl->dihkql", w, pick, precision=lax.Precision.HIGHEST).reshape(1024, 128)
    g, loc, v, tz = exchange(x0, x1, pm, zm, wd, local_weight, bias_term.reshape(1, 16))
    out, tan = inverse(loc, g.reshape(8192, 128), v, tz)
    return out.reshape(16, 4, ZL, FL), tan.reshape(16, 4, ZL, FL)


def solution(mesh):
    return jax.shard_map(
        body,
        mesh=mesh,
        in_specs=(
            P(None, None, "gz", "phi"),
            P(None, None, "gz", "phi"),
            P(None, None, None, "gz", "phi"),
            P(),
            P(),
            P(),
            P(),
        ),
        out_specs=(P(None, None, "gz", "phi"), P(None, None, "gz", "phi")),
        check_vma=False,
    )
```

```python
import functools
import math

import jax
import jax.numpy as jnp
from jax import lax
from jax.experimental import pallas as pl
from jax.experimental.pallas import tpu as pltpu
from jax.sharding import PartitionSpec as P

C, R, ZL, FL = 16, 4, 64, 256
Z, PHI, KZ, KP = 2048, 1024, 64, 64
F32, BF16, I32 = jnp.float32, jnp.bfloat16, jnp.int32
MESH = pl.DeviceIdType.MESH
VMEM_EXCHANGE = 46 << 20
VMEM_INVERSE = 44 << 20
SCALE = (1.0 / math.sqrt(Z * PHI)) * (2.0 / math.sqrt(KZ * KP))


def iota(shape, dim):
    return lax.broadcasted_iota(I32, shape, dim)


def split(x):
    hi = x.astype(BF16)
    return hi, (x - hi.astype(F32)).astype(BF16)


def wave(turns, length):
    quarter = length // 4
    near = ((turns + 2 * quarter) & (length - 1)) - 2 * quarter
    x = (quarter - jnp.abs(near)).astype(F32) * (2.0 * math.pi / length)
    x2 = x * x
    acc = 1.0 / math.factorial(13)
    for n in (11, 9, 7, 5, 3, 1):
        acc = acc * x2 + (1.0 if n % 4 == 1 else -1.0) / math.factorial(n)
    return acc * x


def nt(a, b):
    return lax.dot_general(a, b, (((1,), (1,)), ((), ())), preferred_element_type=F32)


def nn(a, b):
    return jnp.dot(a, b, preferred_element_type=F32)


def pick_column(modes_ref, which):
    hit = iota((128, 64), 1) == which
    return jnp.sum(jnp.where(hit, modes_ref[...].astype(F32), 0.0), axis=1, keepdims=True).astype(I32)


def phi_table(modes_ref):
    row = iota((128, 64), 0)
    col = pick_column(modes_ref, row // 16 * 8 + row % 8)
    f = lax.axis_index("phi") * FL + iota((128, FL), 1)
    return wave(f * col + (iota((128, FL), 0) // 8 % 2) * (PHI // 4), PHI)


def z_table(modes_ref, z, turn):
    row = iota((128, 64), 0)
    col = pick_column(modes_ref, row // 4 % 16 * 4 + row // 64 * 2 + row // 2 % 2)
    return wave((lax.axis_index("gz") * ZL + z) * col + turn, Z)


def places(j):
    q = 2 * j
    base = ((q // 16) * 1024 + (q // 8 % 2) * 128 + q % 8, (q // 8) * 128 + q % 8 + 4096)
    step = (256, 1024)
    return [
        [pl.ds(base[g // 8] + (n + (g % 8 // 2) * step[g // 8] + (g % 2) * 64), 8, stride=8) for g in range(16)]
        for n in range(2)
    ]


def fetch(x0_ref, x1_ref, x_buf, sem, zb):
    copies = []
    for p, src in enumerate((x0_ref, x1_ref)):
        for h in range(2):
            n = zb * 4 + p * 2 + h
            copies.append(pltpu.make_async_copy(
                src.at[:, pl.ds(pl.multiple_of(zb * 8, 8), 8), pl.ds(h * 128, 128)], x_buf.at[n], sem.at[n]
            ))
    return copies


def stack_z(x_buf, zb, i):
    flat = x_buf.reshape(32 * 512, 128)
    a, b, c, d = (flat[pl.ds(zb * 2048 + n * 512 + i, 64, stride=8), :] for n in range(4))
    return jnp.concatenate([jnp.concatenate([a, b], axis=1), jnp.concatenate([c, d], axis=1)], axis=0)


def cat(parts, axis):
    return jnp.concatenate(parts, axis=axis)


def transform(x0_ref, x1_ref, pm_ref, zm_ref, s_ref, x_buf, a_ref, xs_ref, v_ref, sem):
    for zb in range(8):
        for c in fetch(x0_ref, x1_ref, x_buf, sem, zb):
            c.start()
    w_hi, w_lo = split(phi_table(pm_ref))
    w2 = cat([w_hi, w_lo], 0)
    v_ref[...] = w2
    shape = (128, 128)
    turn = (iota(shape, 0) % 2 - iota(shape, 1) // 64) * (Z // 4)
    t_hi, t_lo = split(z_table(zm_ref, iota(shape, 1) % 64, turn))
    t3 = cat([t_hi, t_lo, t_hi], 1)

    def arrive(zb):
        for c in fetch(x0_ref, x1_ref, x_buf, sem, zb):
            c.wait()

    def block(k, carry):
        for n in range(2):
            arrive(2 * k + n)
        for i in range(8):
            base = pl.multiple_of(k * 2048, 2048) + i // 4 * 1024
            base2 = pl.multiple_of(k * 4096, 4096) + i * 512
            for n in range(2):
                hi, lo = split(stack_z(x_buf, 2 * k + i // 4, i % 4 * 2 + n))
                xs_ref[pl.ds(base2 + n * 128, 128), :] = hi
                xs_ref[pl.ds(base2 + (256 + n * 128), 128), :] = lo
            hi = xs_ref[pl.ds(base2, 256), :]
            lo = xs_ref[pl.ds(base2 + 256, 256), :]
            o = nt(w2, hi)
            o = o[:128] + (o[128:] + nt(w_hi, lo))
            for n in range(2):
                a_ref[pl.ds(base + (i % 4 * 2 + n), 128, stride=8), :] = o[:, n * 128 : (n + 1) * 128]
        return carry

    lax.fori_loop(0, 4, block, 0)

    def pair(j, carry):
        base = pl.multiple_of(((j // 4) * 16 + j % 4 * 2) * 8, 16)

        def rows(n):
            return cat([
                a_ref[pl.ds(base + (n * 8 + part * 64 + zb * 1024), 8), :] for part in range(2) for zb in range(8)
            ], 0)

        hi, lo = split(cat([rows(0), rows(1)], 1))
        o = nn(t3, cat([hi, hi, lo], 0))
        spots = places(j)
        for n in range(2):
            for g in range(16):
                s_ref[spots[n][g], :] = o[g * 8 : g * 8 + 8, n * 128 : (n + 1) * 128]
        return carry

    lax.fori_loop(0, 32, pair, 0, unroll=16)


def inverse_z(modes_ref, t_ref):
    row, col = iota((128, 128), 0), iota((128, 128), 1)
    turn = (row % 2 - col % 2) * (Z // 4)
    hi, lo = split(z_table(modes_ref, col // 2, turn).T)
    t_ref[:, 0:128] = hi
    t_ref[:, 128:256] = lo


def local_mixing(lw_ref, bias_ref):
    pick = (iota((128, 16), 0) // 4 % 16 == iota((128, 16), 1)).astype(F32)
    full = lax.Precision.HIGHEST
    rows = lax.dot_general(pick, lw_ref[...], (((1,), (1,)), ((), ())), precision=full, preferred_element_type=F32)
    grid = lax.dot_general(rows, pick, (((1,), (1,)), ((), ())), precision=full, preferred_element_type=F32)
    row, col = iota((128, 128), 0), iota((128, 128), 1)
    same = (row // 64 == col // 64) & (row % 4 == col % 4)
    l_hi, l_lo = split(jnp.where(same, grid, 0.0))
    here = (iota((128, 16), 0) // 4 == iota((128, 16), 1))
    bias = jnp.sum(jnp.where(here, bias_ref[...], 0.0), axis=1, keepdims=True)
    return cat([l_hi, l_lo, l_hi], 1), bias


HBM = pl.BlockSpec(memory_space=pltpu.HBM)
VMEM = pl.BlockSpec(memory_space=pltpu.VMEM)


def mix(x_ref, w_ref, out_ref):
    def pair(ref):
        re = cat([ref[pl.ds(n * 16, 8), :] for n in range(4)], 0)
        im = cat([ref[pl.ds(n * 16 + 8, 8), :] for n in range(4)], 0)
        return re * SCALE, im * SCALE

    xr, xi = pair(x_ref)
    lane = iota((32, 128), 1) % 64
    gr = jnp.zeros((32, 128), F32)
    gi = jnp.zeros((32, 128), F32)
    for d in range(16):
        if d == 0:
            ar, ai = xr, xi
        else:
            near = lane < 64 - 4 * d
            ar = jnp.where(near, pltpu.roll(xr, 128 - 4 * d, 1), pltpu.roll(xr, 64 - 4 * d, 1))
            ai = jnp.where(near, pltpu.roll(xi, 128 - 4 * d, 1), pltpu.roll(xi, 64 - 4 * d, 1))
        wr = w_ref[pl.ds(d * 64, 32), :]
        wi = w_ref[pl.ds(d * 64 + 32, 32), :]
        gr = gr + (ar * wr - ai * wi)
        gi = gi + (ai * wr + ar * wi)
    for n in range(4):
        out_ref[pl.ds(n * 16, 8), :] = gr[n * 8 : n * 8 + 8]
        out_ref[pl.ds(n * 16 + 8, 8), :] = gi[n * 8 : n * 8 + 8]


def exchange_kernel(
    x0_ref, x1_ref, pm_ref, zm_ref, w_ref, lw_ref, bias_ref, g_ref, loc_ref, v_ref, t_ref,
    x_buf, a_ref, xs_ref, spec_ref, loc_buf, x_sem, loc_sem, peer, acc, relay, fin, second, relay2, rec2, third, rec3, own, gath3,
    pair_s, pair_r, st1_s, st1_r, st2_s, st2_r, st3_s, st3_r,
    ag3_s, ag3_r, ag2_s, ag2_r, ag1_s, ag1_r, hand_s, hand_r,
):
    gz = lax.axis_index("gz")
    x = lax.axis_index("phi")
    core = gz % 2
    z = (gz // 2) % 4
    y = gz // 8

    def device(xx, yy, zz, cc):
        return ((yy * 4 + zz) * 2 + cc, xx)

    pa = x + core * (y - x)
    pb = z
    pd = y + core * (x - y)

    def along_a(t):
        n = (pa + t) % 4
        return device(n + core * (x - n), y + core * (n - y), z, core)

    def along_b(t):
        return device(x, y, (z + t) % 4, core)

    def along_d(t):
        n = (pd + t) % 4
        return device(x + core * (n - x), n + core * (y - n), z, core)

    partner = device(x, y, z, 1 - core)

    sent = []

    def send(src, dst, ss, rs, dev):
        c = pltpu.make_async_remote_copy(
            src_ref=src, dst_ref=dst, send_sem=ss, recv_sem=rs, device_id=dev, device_id_type=MESH
        )
        c.start()
        sent.append(c)
        return c

    right, left = along_a(1), along_a(3)
    barrier = pltpu.get_barrier_semaphore()
    peers = [partner, right, left]
    peers += [along_b(1), along_b(3)] + [along_d(t) for t in (1, 2, 3)]
    for dev in peers:
        pl.semaphore_signal(barrier, inc=1, device_id=dev, device_id_type=MESH)
    transform(x0_ref, x1_ref, pm_ref, zm_ref, spec_ref, x_buf, a_ref, xs_ref, v_ref, x_sem)
    s_ref = spec_ref.reshape(2, 4, 8, 4, 32, 128)
    pl.semaphore_wait(barrier, 8)

    def mine(t):
        return (pa + t) % 4

    qa = y + core * (x - y)
    order = (2, 1, 3, 0)
    pairs = []
    for n, t in enumerate(order):
        pairs.append(send(s_ref.at[1 - core, (qa + t) % 4], peer.at[n], pair_s.at[n], pair_r.at[n], partner))

    l3, bias = local_mixing(lw_ref, bias_ref)
    stores = []

    def mix_local(zb):
        slot = zb % 2
        if zb >= 2:
            stores[zb - 2].wait()

        def four(i, carry):
            for n in range(4):
                row = (zb * 4 + n // 2) * 512 + n % 2 * 128
                hi = xs_ref[pl.ds(pl.multiple_of(i * 1024 + row, 128), 128), :]
                lo = xs_ref[pl.ds(pl.multiple_of(i * 1024 + row + 256, 128), 128), :]
                o = nn(l3, cat([hi, hi, lo], 0)) + bias
                loc_buf[slot, pl.ds(pl.multiple_of(i * 512 + n * 128, 128), 128), :] = o
            return carry

        lax.fori_loop(0, 2, four, 0)
        c = pltpu.make_async_copy(loc_buf.at[slot], loc_ref.at[pl.ds(zb * 1024, 1024), :], loc_sem.at[zb])
        c.start()
        stores.append(c)

    mix_local(0)

    def land(n):
        pairs[n].wait_recv()
        acc[n] = s_ref[core, mine(order[n])] + peer[n]

    def piece(slab, s, h, size=4):
        return acc.at[slab, pl.ds(h * 4, size), (pb + s) % 4]

    turns = (2, 1, 3, 0)
    land(0)
    relays = {}
    for s in turns:
        n = s * 6
        relays[0, s] = send(piece(0, s, 0), relay.at[0, s], st1_s.at[n], st1_r.at[n], right)
        relays[1, s] = send(piece(0, s, 1), relay.at[1, s], st1_s.at[n + 1], st1_r.at[n + 1], left)
    mix_local(1)
    land(1)
    land(2)
    first = {}
    for s in turns:
        n = s * 6
        first[s] = [
            send(piece(1, s, 1), fin.at[0, s, pl.ds(4, 4)], st1_s.at[n + 2], st1_r.at[n + 2], right),
            send(piece(2, s, 0), fin.at[1, s, pl.ds(0, 4)], st1_s.at[n + 3], st1_r.at[n + 3], left),
        ]
        mix_local(2 + turns.index(s))
        for side, dev in enumerate((right, left)):
            relays[side, s].wait_recv()
            ref = piece(1 + side, s, side)
            ref[...] = ref[...] + relay[side, s]
            dst = fin.at[side, s, pl.ds(side * 4, 4)]
            first[s].append(send(ref, dst, st1_s.at[n + 4 + side], st1_r.at[n + 4 + side], dev))
    land(3)

    sends2 = []
    for s in turns:
        for c in first[s]:
            c.wait_recv()
        second[s] = piece(3, s, 0, 8)[...] + (fin[0, s] + fin[1, s])
        if s == 2:
            far = [
                send(second.at[2, pl.ds(h * 4, 4)], relay2.at[h], st2_s.at[h], st2_r.at[h], along_b(1 + 2 * h))
                for h in range(2)
            ]
        elif s:
            h = s // 2
            far[h].wait_recv()
            part = second.at[s, pl.ds(h * 4, 4)]
            part[...] = part[...] + relay2[h]
            sends2.append(send(second.at[s], rec2.at[h], st2_s.at[2 + h], st2_r.at[2 + h], along_b(s)))
    mix_local(6)
    for c in sends2:
        c.wait_recv()
    third[...] = (second[0] + (rec2[0] + rec2[1])).reshape(4, 64, 128)

    sends3 = []
    for t in turns[:3]:
        sends3.append(send(third.at[(pd + t) % 4], rec3.at[t - 1], st3_s.at[t - 1], st3_r.at[t - 1], along_d(t)))
    mix_local(7)
    for c in sends3:
        c.wait_recv()
    own[...] = third[pd] + rec3[0] + (rec3[1] + rec3[2])
    mine3 = gath3.at[pd]
    mix(own, w_ref, mine3)

    gat3 = [send(mine3, mine3, ag3_s.at[t - 1], ag3_r.at[t - 1], along_d(t)) for t in turns[:3]]
    inverse_z(zm_ref, t_ref)
    for c in gat3:
        c.wait_recv()

    def spot(t, s, h, size=4):
        return g_ref.at[core, mine(t), pl.ds(h * 4, size), (pb + s) % 4]

    mine2 = spot(0, 0, 0, 8)
    mine2[...] = gath3[...].reshape(8, 32, 128)

    gat2, gat1, hands = {}, {}, []

    def pass_b(key, u, h, t):
        n = ("ra", "lb", "rb", "la", "fr", "fl").index(key)
        gat2[key] = send(spot(0, u, h), spot(0, u, h), ag2_s.at[n], ag2_r.at[n], along_b(t))

    def pass_a(key, u, t, h, dev):
        n = u * 6 + ("ra", "lb", "rb", "la", "fr", "fl").index(key)
        gat1[u, key] = send(spot(t, u, h), spot(t, u, h), ag1_s.at[n], ag1_r.at[n], dev)

    def hand(u, n, t, h):
        ref = spot(t, u, h)
        hands.append(send(ref, ref, hand_s.at[u * 8 + n], hand_r.at[u * 8 + n], partner))

    def emit(u, h):
        if h == 0:
            pass_a("ra", u, 0, 0, right)
            pass_a("la", u, 0, 0, left)
        else:
            pass_a("lb", u, 0, 1, left)
            pass_a("rb", u, 0, 1, right)
        hand(u, h, 0, h)

    def turn_round(u):
        gat1[u, "ra"].wait_recv()
        pass_a("fr", u, 3, 0, right)
        gat1[u, "lb"].wait_recv()
        pass_a("fl", u, 1, 1, left)
        hand(u, 2, 3, 0)
        hand(u, 3, 1, 1)

    pass_b("ra", 0, 0, 1)
    pass_b("lb", 0, 1, 3)
    pass_b("rb", 0, 1, 1)
    pass_b("la", 0, 0, 3)
    emit(0, 0)
    emit(0, 1)
    gat2["ra"].wait_recv()
    pass_b("fr", 3, 0, 1)
    gat2["lb"].wait_recv()
    pass_b("fl", 1, 1, 3)
    emit(3, 0)
    emit(1, 1)
    turn_round(0)
    gat2["rb"].wait_recv()
    emit(3, 1)
    gat2["la"].wait_recv()
    emit(1, 0)
    gat2["fr"].wait_recv()
    emit(2, 0)
    gat2["fl"].wait_recv()
    emit(2, 1)
    for u in (3, 1, 2):
        turn_round(u)
    for u in (0, 3, 1, 2):
        gat1[u, "rb"].wait_recv()
        hand(u, 4, 3, 1)
        gat1[u, "la"].wait_recv()
        hand(u, 5, 1, 0)
        gat1[u, "fr"].wait_recv()
        hand(u, 6, 2, 0)
        gat1[u, "fl"].wait_recv()
        hand(u, 7, 2, 1)
    for c in hands:
        c.wait_recv()
    for c in sent:
        c.wait_send()
    for c in stores[6:]:
        c.wait()


def exchange(field, field_tangent, pm, zm, wt, lw, bias):
    dma = pltpu.SemaphoreType.DMA
    buf = lambda *dims: pltpu.VMEM((*dims, 128), F32)
    table = jax.ShapeDtypeStruct((256, 256), BF16)
    return pl.pallas_call(
        exchange_kernel,
        out_shape=(
            jax.ShapeDtypeStruct((2, 4, 8, 4, 32, 128), F32), jax.ShapeDtypeStruct((8192, FL), F32),
            table, jax.ShapeDtypeStruct((128, 256), BF16),
        ),
        in_specs=[HBM, HBM, VMEM, VMEM, VMEM, VMEM, VMEM],
        out_specs=(VMEM, HBM, VMEM, VMEM),
        scratch_shapes=[
            buf(32, 64, 8), buf(8192), pltpu.VMEM((16384, FL), BF16), buf(8192),
            pltpu.VMEM((2, 1024, FL), F32), dma((32,)), dma((8,)),
            buf(4, 8, 4, 32), buf(4, 8, 4, 32), buf(2, 4, 4, 32), buf(2, 4, 8, 32), buf(4, 8, 32), buf(2, 4, 32), buf(2, 8, 32),
            buf(4, 64), buf(3, 64), buf(64), buf(4, 64),
            dma((4,)), dma((4,)), dma((24,)), dma((24,)), dma((4,)), dma((4,)), dma((3,)), dma((3,)),
            dma((3,)), dma((3,)), dma((6,)), dma((6,)), dma((24,)), dma((24,)), dma((32,)), dma((32,)),
        ],
        compiler_params=pltpu.CompilerParams(collective_id=0, has_side_effects=True, vmem_limit_bytes=VMEM_EXCHANGE),
        name="exchange_kernel",
    )(field, field_tangent, pm, zm, wt, lw, bias)


def inverse_kernel(
    loc_hbm, g_ref, v_ref, tz_ref, o_ref, t_ref, loc_ref, u_ref, acc_ref, out_buf, loc_sem, out_sem
):
    def take(zb):
        rows = pl.ds(pl.multiple_of(zb * 1024, 1024), 1024)
        return pltpu.make_async_copy(loc_hbm.at[rows, :], loc_ref.at[rows, :], loc_sem.at[zb])

    for zb in range(8):
        take(zb).start()
    t_hi, t_lo = tz_ref[:, 0:128], tz_ref[:, 128:256]
    t3 = cat([t_hi, t_lo, t_hi], 1)

    def pair(j, carry):
        spots = places(j)
        g2 = cat([cat([g_ref[spots[n][g], :] for g in range(16)], 0) for n in range(2)], 1)
        hi, lo = split(g2)
        o = nn(t3, cat([hi, hi, lo], 0))
        base = (j // 4) * 1024 + j % 4 * 2
        for n in range(2):
            for g in range(16):
                u_ref[pl.ds(base + (n + g * 64), 8, stride=8), :] = o[g * 8 : g * 8 + 8, n * 128 : (n + 1) * 128]
        return carry

    lax.fori_loop(0, 32, pair, 0, unroll=16)
    v_hi, v_lo = v_ref[0:128, :], v_ref[128:256, :]
    v3 = cat([v_hi, v_hi, v_lo], 0)
    c0 = math.sqrt(2.0 / math.pi)

    def copies(zb, slot):
        out = []
        for n, dst in enumerate((o_ref, t_ref)):
            for h in range(2):
                out.append(pltpu.make_async_copy(
                    out_buf.at[slot * 4 + n * 2 + h], dst.at[:, pl.ds(pl.multiple_of(zb * 8, 8), 8), pl.ds(h * 128, 128)],
                    out_sem.at[slot * 4 + n * 2 + h],
                ))
        return out

    def gather_z(z, slot):
        z16 = z * 16
        u = cat([u_ref[pl.ds(pl.multiple_of(n * 1024 + z16, 16), 16), :] for n in range(8)], 0)
        u_hi, u_lo = split(u.T)
        local = loc_ref[pl.ds(pl.multiple_of(z * 128, 128), 128), :]
        acc_ref[slot] = nn(cat([u_hi, u_lo, u_hi], 1), v3) + local

    take(0).wait()
    gather_z(0, 0)

    def block(k, carry):
        take(2 * k + 1).wait()

        @pl.when(k < 3)
        def _():
            take(2 * k + 2).wait()

        @pl.when(k >= 1)
        def _():
            for n in range(2):
                for c in copies(2 * k + n, n):
                    c.wait()

        flat = out_buf.reshape(8 * 512, 128)
        for slot in range(2):
            zb = 2 * k + slot
            for i in range(8):
                gather_z(jnp.minimum(zb * 8 + i + 1, 63), (i + 1) % 2)
                pre = acc_ref[i % 2, 0:64, :]
                tan = acc_ref[i % 2, 64:128, :]
                sq = pre * pre
                t = jnp.tanh(pre * (c0 + (c0 * 0.044715) * sq))
                half = 0.5 + 0.5 * t
                res = pre * half
                slope = half + res * ((1.0 - t) * (c0 + (3.0 * 0.044715 * c0) * sq))
                for n, val in enumerate((res, slope * tan)):
                    for h in range(2):
                        flat[pl.ds(slot * 2048 + n * 1024 + h * 512 + i, 64, stride=8), :] = val[:, h * 128 : (h + 1) * 128]
            for c in copies(zb, slot):
                c.start()
        return carry

    lax.fori_loop(0, 4, block, 0)
    for zb in (6, 7):
        for c in copies(zb, zb % 2):
            c.wait()


def inverse(loc, g, v, tz):
    out = jax.ShapeDtypeStruct((64, ZL, FL), F32)
    return pl.pallas_call(
        inverse_kernel,
        out_shape=(out, out),
        in_specs=[HBM, VMEM, VMEM, VMEM],
        out_specs=(HBM, HBM),
        scratch_shapes=[
            pltpu.VMEM((8192, FL), F32), pltpu.VMEM((8192, 128), F32), pltpu.VMEM((2, 128, FL), F32), pltpu.VMEM((8, 64, 8, 128), F32),
            pltpu.SemaphoreType.DMA((8,)), pltpu.SemaphoreType.DMA((8,)),
        ],
        compiler_params=pltpu.CompilerParams(vmem_limit_bytes=VMEM_INVERSE),
        name="inverse_kernel",
    )(loc, g, v, tz)


def body(field, field_tangent, spectral_weight, local_weight, bias_term, z_modes, phi_modes):
    x0 = field.reshape(64, ZL, FL)
    x1 = field_tangent.reshape(64, ZL, FL)
    zm = z_modes.reshape(1, 64)
    pm = phi_modes.reshape(1, 64)
    w = spectral_weight.reshape(2, 16, 16, 2, 2, 8)
    c, o, d, lane = (lax.broadcasted_iota(I32, (16, 16, 16, 128), n) for n in range(4))
    lane_o = lane // 4 % 16
    pick = ((o == lane_o) & (c == (lane_o + d) % 16)).astype(F32)
    wd = jnp.einsum("icokhq,codl->dihkql", w, pick, precision=lax.Precision.HIGHEST).reshape(1024, 128)
    g, loc, v, tz = exchange(x0, x1, pm, zm, wd, local_weight, bias_term.reshape(1, 16))
    out, tan = inverse(loc, g.reshape(8192, 128), v, tz)
    return out.reshape(16, 4, ZL, FL), tan.reshape(16, 4, ZL, FL)


def solution(mesh):
    return jax.shard_map(
        body,
        mesh=mesh,
        in_specs=(
            P(None, None, "gz", "phi"),
            P(None, None, "gz", "phi"),
            P(None, None, None, "gz", "phi"),
            P(),
            P(),
            P(),
            P(),
        ),
        out_specs=(P(None, None, "gz", "phi"), P(None, None, "gz", "phi")),
        check_vma=False,
    )
```

```python
import functools
import math

import jax
import jax.numpy as jnp
from jax import lax
from jax.experimental import pallas as pl
from jax.experimental.pallas import tpu as pltpu
from jax.sharding import PartitionSpec as P

C, R, ZL, FL = 16, 4, 64, 256
Z, PHI, KZ, KP = 2048, 1024, 64, 64
F32, BF16, I32 = jnp.float32, jnp.bfloat16, jnp.int32
MESH = pl.DeviceIdType.MESH
VMEM_EXCHANGE = 46 << 20
VMEM_INVERSE = 44 << 20
SCALE = (1.0 / math.sqrt(Z * PHI)) * (2.0 / math.sqrt(KZ * KP))


def iota(shape, dim):
    return lax.broadcasted_iota(I32, shape, dim)


def split(x):
    hi = x.astype(BF16)
    return hi, (x - hi.astype(F32)).astype(BF16)


def wave(turns, length):
    quarter = length // 4
    near = ((turns + 2 * quarter) & (length - 1)) - 2 * quarter
    x = (quarter - jnp.abs(near)).astype(F32) * (2.0 * math.pi / length)
    x2 = x * x
    acc = 1.0 / math.factorial(13)
    for n in (11, 9, 7, 5, 3, 1):
        acc = acc * x2 + (1.0 if n % 4 == 1 else -1.0) / math.factorial(n)
    return acc * x


def nt(a, b):
    return lax.dot_general(a, b, (((1,), (1,)), ((), ())), preferred_element_type=F32)


def nn(a, b):
    return jnp.dot(a, b, preferred_element_type=F32)


def pick_column(modes_ref, which):
    hit = iota((128, 64), 1) == which
    return jnp.sum(jnp.where(hit, modes_ref[...].astype(F32), 0.0), axis=1, keepdims=True).astype(I32)


def phi_table(modes_ref):
    row = iota((128, 64), 0)
    col = pick_column(modes_ref, row // 16 * 8 + row % 8)
    f = lax.axis_index("phi") * FL + iota((128, FL), 1)
    return wave(f * col + (iota((128, FL), 0) // 8 % 2) * (PHI // 4), PHI)


def z_table(modes_ref, z, turn):
    row = iota((128, 64), 0)
    col = pick_column(modes_ref, row // 4 % 16 * 4 + row // 64 * 2 + row // 2 % 2)
    return wave((lax.axis_index("gz") * ZL + z) * col + turn, Z)


def places(j):
    q = 2 * j
    base = ((q // 16) * 1024 + (q // 8 % 2) * 128 + q % 8, (q // 8) * 128 + q % 8 + 4096)
    step = (256, 1024)
    return [
        [pl.ds(base[g // 8] + (n + (g % 8 // 2) * step[g // 8] + (g % 2) * 64), 8, stride=8) for g in range(16)]
        for n in range(2)
    ]


def fetch(x0_ref, x1_ref, x_buf, sem, zb):
    copies = []
    for p, src in enumerate((x0_ref, x1_ref)):
        for h in range(2):
            n = zb * 4 + p * 2 + h
            copies.append(pltpu.make_async_copy(
                src.at[:, pl.ds(pl.multiple_of(zb * 8, 8), 8), pl.ds(h * 128, 128)], x_buf.at[n], sem.at[n]
            ))
    return copies


def stack_z(x_buf, zb, i):
    flat = x_buf.reshape(32 * 512, 128)
    a, b, c, d = (flat[pl.ds(zb * 2048 + n * 512 + i, 64, stride=8), :] for n in range(4))
    return jnp.concatenate([jnp.concatenate([a, b], axis=1), jnp.concatenate([c, d], axis=1)], axis=0)


def cat(parts, axis):
    return jnp.concatenate(parts, axis=axis)


def transform(x0_ref, x1_ref, pm_ref, zm_ref, s_ref, x_buf, a_ref, xs_ref, v_ref, sem):
    for zb in range(8):
        for c in fetch(x0_ref, x1_ref, x_buf, sem, zb):
            c.start()
    w_hi, w_lo = split(phi_table(pm_ref))
    w2 = cat([w_hi, w_lo], 0)
    v_ref[...] = w2
    shape = (128, 128)
    turn = (iota(shape, 0) % 2 - iota(shape, 1) // 64) * (Z // 4)
    t_hi, t_lo = split(z_table(zm_ref, iota(shape, 1) % 64, turn))
    t3 = cat([t_hi, t_lo, t_hi], 1)

    def arrive(zb):
        for c in fetch(x0_ref, x1_ref, x_buf, sem, zb):
            c.wait()

    def block(k, carry):
        for n in range(2):
            arrive(2 * k + n)
        for i in range(8):
            base = pl.multiple_of(k * 2048, 2048) + i // 4 * 1024
            base2 = pl.multiple_of(k * 4096, 4096) + i * 512
            for n in range(2):
                hi, lo = split(stack_z(x_buf, 2 * k + i // 4, i % 4 * 2 + n))
                xs_ref[pl.ds(base2 + n * 128, 128), :] = hi
                xs_ref[pl.ds(base2 + (256 + n * 128), 128), :] = lo
            hi = xs_ref[pl.ds(base2, 256), :]
            lo = xs_ref[pl.ds(base2 + 256, 256), :]
            o = nt(w2, hi)
            o = o[:128] + (o[128:] + nt(w_hi, lo))
            for n in range(2):
                a_ref[pl.ds(base + (i % 4 * 2 + n), 128, stride=8), :] = o[:, n * 128 : (n + 1) * 128]
        return carry

    lax.fori_loop(0, 4, block, 0)

    def pair(j, carry):
        base = pl.multiple_of(((j // 4) * 16 + j % 4 * 2) * 8, 16)

        def rows(n):
            return cat([
                a_ref[pl.ds(base + (n * 8 + part * 64 + zb * 1024), 8), :] for part in range(2) for zb in range(8)
            ], 0)

        hi, lo = split(cat([rows(0), rows(1)], 1))
        o = nn(t3, cat([hi, hi, lo], 0))
        spots = places(j)
        for n in range(2):
            for g in range(16):
                s_ref[spots[n][g], :] = o[g * 8 : g * 8 + 8, n * 128 : (n + 1) * 128]
        return carry

    lax.fori_loop(0, 32, pair, 0, unroll=16)


def inverse_z(modes_ref, t_ref):
    row, col = iota((128, 128), 0), iota((128, 128), 1)
    turn = (row % 2 - col % 2) * (Z // 4)
    hi, lo = split(z_table(modes_ref, col // 2, turn).T)
    t_ref[:, 0:128] = hi
    t_ref[:, 128:256] = lo


def local_mixing(lw_ref, bias_ref):
    pick = (iota((128, 16), 0) // 4 % 16 == iota((128, 16), 1)).astype(F32)
    full = lax.Precision.HIGHEST
    rows = lax.dot_general(pick, lw_ref[...], (((1,), (1,)), ((), ())), precision=full, preferred_element_type=F32)
    grid = lax.dot_general(rows, pick, (((1,), (1,)), ((), ())), precision=full, preferred_element_type=F32)
    row, col = iota((128, 128), 0), iota((128, 128), 1)
    same = (row // 64 == col // 64) & (row % 4 == col % 4)
    l_hi, l_lo = split(jnp.where(same, grid, 0.0))
    here = (iota((128, 16), 0) // 4 == iota((128, 16), 1))
    bias = jnp.sum(jnp.where(here, bias_ref[...], 0.0), axis=1, keepdims=True)
    return cat([l_hi, l_lo, l_hi], 1), bias


HBM = pl.BlockSpec(memory_space=pltpu.HBM)
VMEM = pl.BlockSpec(memory_space=pltpu.VMEM)


def mix(x_ref, w_ref, out_ref):
    def pair(ref):
        re = cat([ref[pl.ds(n * 16, 8), :] for n in range(4)], 0)
        im = cat([ref[pl.ds(n * 16 + 8, 8), :] for n in range(4)], 0)
        return re * SCALE, im * SCALE

    xr, xi = pair(x_ref)
    lane = iota((32, 128), 1) % 64
    gr = jnp.zeros((32, 128), F32)
    gi = jnp.zeros((32, 128), F32)
    for d in range(16):
        if d == 0:
            ar, ai = xr, xi
        else:
            near = lane < 64 - 4 * d
            ar = jnp.where(near, pltpu.roll(xr, 128 - 4 * d, 1), pltpu.roll(xr, 64 - 4 * d, 1))
            ai = jnp.where(near, pltpu.roll(xi, 128 - 4 * d, 1), pltpu.roll(xi, 64 - 4 * d, 1))
        wr = w_ref[pl.ds(d * 64, 32), :]
        wi = w_ref[pl.ds(d * 64 + 32, 32), :]
        gr = gr + (ar * wr - ai * wi)
        gi = gi + (ai * wr + ar * wi)
    for n in range(4):
        out_ref[pl.ds(n * 16, 8), :] = gr[n * 8 : n * 8 + 8]
        out_ref[pl.ds(n * 16 + 8, 8), :] = gi[n * 8 : n * 8 + 8]


def exchange_kernel(
    x0_ref, x1_ref, pm_ref, zm_ref, w_ref, lw_ref, bias_ref, g_ref, loc_ref, v_ref, t_ref,
    x_buf, a_ref, xs_ref, spec_ref, loc_buf, x_sem, loc_sem, peer, acc, relay, fin, second, relay2, rec2, third, rec3, own, gath3,
    pair_s, pair_r, st1_s, st1_r, st2_s, st2_r, st3_s, st3_r,
    ag3_s, ag3_r, ag2_s, ag2_r, ag1_s, ag1_r, hand_s, hand_r,
):
    gz = lax.axis_index("gz")
    x = lax.axis_index("phi")
    core = gz % 2
    z = (gz // 2) % 4
    y = gz // 8

    def device(xx, yy, zz, cc):
        return ((yy * 4 + zz) * 2 + cc, xx)

    pa = x + core * (y - x)
    pb = z
    pd = y + core * (x - y)

    def along_a(t):
        n = (pa + t) % 4
        return device(n + core * (x - n), y + core * (n - y), z, core)

    def along_b(t):
        return device(x, y, (z + t) % 4, core)

    def along_d(t):
        n = (pd + t) % 4
        return device(x + core * (n - x), n + core * (y - n), z, core)

    partner = device(x, y, z, 1 - core)

    sent = []

    def send(src, dst, ss, rs, dev):
        c = pltpu.make_async_remote_copy(
            src_ref=src, dst_ref=dst, send_sem=ss, recv_sem=rs, device_id=dev, device_id_type=MESH
        )
        c.start()
        sent.append(c)
        return c

    right, left = along_a(1), along_a(3)
    barrier = pltpu.get_barrier_semaphore()
    peers = [partner, right, left]
    peers += [along_b(1), along_b(3)] + [along_d(t) for t in (1, 2, 3)]
    for dev in peers:
        pl.semaphore_signal(barrier, inc=1, device_id=dev, device_id_type=MESH)
    transform(x0_ref, x1_ref, pm_ref, zm_ref, spec_ref, x_buf, a_ref, xs_ref, v_ref, x_sem)
    s_ref = spec_ref.reshape(2, 4, 8, 4, 32, 128)
    pl.semaphore_wait(barrier, 8)

    def mine(t):
        return (pa + t) % 4

    qa = y + core * (x - y)
    order = (2, 1, 3, 0)
    pairs = []
    for n, t in enumerate(order):
        pairs.append(send(s_ref.at[1 - core, (qa + t) % 4], peer.at[n], pair_s.at[n], pair_r.at[n], partner))

    l3, bias = local_mixing(lw_ref, bias_ref)
    stores = []

    def mix_local(zb):
        slot = zb % 2
        if zb >= 2:
            stores[zb - 2].wait()

        def four(i, carry):
            for n in range(4):
                row = (zb * 4 + n // 2) * 512 + n % 2 * 128
                hi = xs_ref[pl.ds(pl.multiple_of(i * 1024 + row, 128), 128), :]
                lo = xs_ref[pl.ds(pl.multiple_of(i * 1024 + row + 256, 128), 128), :]
                o = nn(l3, cat([hi, hi, lo], 0)) + bias
                loc_buf[slot, pl.ds(pl.multiple_of(i * 512 + n * 128, 128), 128), :] = o
            return carry

        lax.fori_loop(0, 2, four, 0)
        c = pltpu.make_async_copy(loc_buf.at[slot], loc_ref.at[pl.ds(zb * 1024, 1024), :], loc_sem.at[zb])
        c.start()
        stores.append(c)

    mix_local(0)

    def land(n):
        pairs[n].wait_recv()
        acc[n] = s_ref[core, mine(order[n])] + peer[n]

    def piece(slab, s, h, size=4):
        return acc.at[slab, pl.ds(h * 4, size), (pb + s) % 4]

    turns = (2, 1, 3, 0)
    land(0)
    relays = {}
    for s in turns:
        n = s * 6
        relays[0, s] = send(piece(0, s, 0), relay.at[0, s], st1_s.at[n], st1_r.at[n], right)
        relays[1, s] = send(piece(0, s, 1), relay.at[1, s], st1_s.at[n + 1], st1_r.at[n + 1], left)
    mix_local(1)
    land(1)
    land(2)
    first = {}
    for s in turns:
        n = s * 6
        first[s] = [
            send(piece(1, s, 1), fin.at[0, s, pl.ds(4, 4)], st1_s.at[n + 2], st1_r.at[n + 2], right),
            send(piece(2, s, 0), fin.at[1, s, pl.ds(0, 4)], st1_s.at[n + 3], st1_r.at[n + 3], left),
        ]
        mix_local(2 + turns.index(s))
        for side, dev in enumerate((right, left)):
            relays[side, s].wait_recv()
            ref = piece(1 + side, s, side)
            ref[...] = ref[...] + relay[side, s]
            dst = fin.at[side, s, pl.ds(side * 4, 4)]
            first[s].append(send(ref, dst, st1_s.at[n + 4 + side], st1_r.at[n + 4 + side], dev))
    land(3)

    sends2 = []
    for s in turns:
        for c in first[s]:
            c.wait_recv()
        second[s] = piece(3, s, 0, 8)[...] + (fin[0, s] + fin[1, s])
        if s == 2:
            far = [
                send(second.at[2, pl.ds(h * 4, 4)], relay2.at[h], st2_s.at[h], st2_r.at[h], along_b(1 + 2 * h))
                for h in range(2)
            ]
        elif s:
            h = s // 2
            far[h].wait_recv()
            part = second.at[s, pl.ds(h * 4, 4)]
            part[...] = part[...] + relay2[h]
            sends2.append(send(second.at[s], rec2.at[h], st2_s.at[2 + h], st2_r.at[2 + h], along_b(s)))
    mix_local(6)
    for c in sends2:
        c.wait_recv()
    third[...] = (second[0] + (rec2[0] + rec2[1])).reshape(4, 64, 128)

    sends3 = []
    for t in turns[:3]:
        sends3.append(send(third.at[(pd + t) % 4], rec3.at[t - 1], st3_s.at[t - 1], st3_r.at[t - 1], along_d(t)))
    mix_local(7)
    for c in sends3:
        c.wait_recv()
    own[...] = third[pd] + rec3[0] + (rec3[1] + rec3[2])
    mine3 = gath3.at[pd]
    mix(own, w_ref, mine3)

    gat3 = [send(mine3, mine3, ag3_s.at[t - 1], ag3_r.at[t - 1], along_d(t)) for t in turns[:3]]
    inverse_z(zm_ref, t_ref)
    for c in gat3:
        c.wait_recv()

    def spot(t, s, h, size=4):
        return g_ref.at[core, mine(t), pl.ds(h * 4, size), (pb + s) % 4]

    mine2 = spot(0, 0, 0, 8)
    mine2[...] = gath3[...].reshape(8, 32, 128)

    gat2, gat1, hands = {}, {}, []

    def pass_b(key, u, h, t):
        n = ("ra", "lb", "rb", "la", "fr", "fl").index(key)
        gat2[key] = send(spot(0, u, h), spot(0, u, h), ag2_s.at[n], ag2_r.at[n], along_b(t))

    def pass_a(key, u, t, h, dev):
        n = u * 6 + ("ra", "lb", "rb", "la", "fr", "fl").index(key)
        gat1[u, key] = send(spot(t, u, h), spot(t, u, h), ag1_s.at[n], ag1_r.at[n], dev)

    def hand(u, n, t, h):
        ref = spot(t, u, h)
        hands.append(send(ref, ref, hand_s.at[u * 8 + n], hand_r.at[u * 8 + n], partner))

    def emit(u, h):
        if h == 0:
            pass_a("ra", u, 0, 0, right)
            pass_a("la", u, 0, 0, left)
        else:
            pass_a("lb", u, 0, 1, left)
            pass_a("rb", u, 0, 1, right)
        hand(u, h, 0, h)

    def turn_round(u):
        gat1[u, "ra"].wait_recv()
        pass_a("fr", u, 3, 0, right)
        gat1[u, "lb"].wait_recv()
        pass_a("fl", u, 1, 1, left)
        hand(u, 2, 3, 0)
        hand(u, 3, 1, 1)

    pass_b("ra", 0, 0, 1)
    pass_b("lb", 0, 1, 3)
    pass_b("rb", 0, 1, 1)
    pass_b("la", 0, 0, 3)
    emit(0, 0)
    emit(0, 1)
    gat2["ra"].wait_recv()
    pass_b("fr", 3, 0, 1)
    gat2["lb"].wait_recv()
    pass_b("fl", 1, 1, 3)
    emit(3, 0)
    emit(1, 1)
    turn_round(0)
    gat2["rb"].wait_recv()
    emit(3, 1)
    gat2["la"].wait_recv()
    emit(1, 0)
    gat2["fr"].wait_recv()
    emit(2, 0)
    gat2["fl"].wait_recv()
    emit(2, 1)
    for u in (3, 1, 2):
        turn_round(u)
    for u in (0, 3, 1, 2):
        gat1[u, "rb"].wait_recv()
        hand(u, 4, 3, 1)
        gat1[u, "la"].wait_recv()
        hand(u, 5, 1, 0)
        gat1[u, "fr"].wait_recv()
        hand(u, 6, 2, 0)
        gat1[u, "fl"].wait_recv()
        hand(u, 7, 2, 1)
    for c in hands:
        c.wait_recv()
    for c in sent:
        c.wait_send()
    for c in stores[6:]:
        c.wait()


def exchange(field, field_tangent, pm, zm, wt, lw, bias):
    dma = pltpu.SemaphoreType.DMA
    buf = lambda *dims: pltpu.VMEM((*dims, 128), F32)
    table = jax.ShapeDtypeStruct((256, 256), BF16)
    return pl.pallas_call(
        exchange_kernel,
        out_shape=(
            jax.ShapeDtypeStruct((2, 4, 8, 4, 32, 128), F32), jax.ShapeDtypeStruct((8192, FL), F32),
            table, jax.ShapeDtypeStruct((128, 256), BF16),
        ),
        in_specs=[HBM, HBM, VMEM, VMEM, VMEM, VMEM, VMEM],
        out_specs=(VMEM, HBM, VMEM, VMEM),
        scratch_shapes=[
            buf(32, 64, 8), buf(8192), pltpu.VMEM((16384, FL), BF16), buf(8192),
            pltpu.VMEM((2, 1024, FL), F32), dma((32,)), dma((8,)),
            buf(4, 8, 4, 32), buf(4, 8, 4, 32), buf(2, 4, 4, 32), buf(2, 4, 8, 32), buf(4, 8, 32), buf(2, 4, 32), buf(2, 8, 32),
            buf(4, 64), buf(3, 64), buf(64), buf(4, 64),
            dma((4,)), dma((4,)), dma((24,)), dma((24,)), dma((4,)), dma((4,)), dma((3,)), dma((3,)),
            dma((3,)), dma((3,)), dma((6,)), dma((6,)), dma((24,)), dma((24,)), dma((32,)), dma((32,)),
        ],
        compiler_params=pltpu.CompilerParams(collective_id=0, has_side_effects=True, vmem_limit_bytes=VMEM_EXCHANGE),
        name="exchange_kernel",
    )(field, field_tangent, pm, zm, wt, lw, bias)


def inverse_kernel(
    loc_hbm, g_ref, v_ref, tz_ref, o_ref, t_ref, loc_ref, u_ref, acc_ref, out_buf, loc_sem, out_sem
):
    def take(zb):
        rows = pl.ds(pl.multiple_of(zb * 1024, 1024), 1024)
        return pltpu.make_async_copy(loc_hbm.at[rows, :], loc_ref.at[rows, :], loc_sem.at[zb])

    for zb in range(8):
        take(zb).start()
    t_hi, t_lo = tz_ref[:, 0:128], tz_ref[:, 128:256]
    t3 = cat([t_hi, t_lo, t_hi], 1)

    def pair(j, carry):
        spots = places(j)
        g2 = cat([cat([g_ref[spots[n][g], :] for g in range(16)], 0) for n in range(2)], 1)
        hi, lo = split(g2)
        o = nn(t3, cat([hi, hi, lo], 0))
        base = (j // 4) * 1024 + j % 4 * 2
        for n in range(2):
            for g in range(16):
                u_ref[pl.ds(base + (n + g * 64), 8, stride=8), :] = o[g * 8 : g * 8 + 8, n * 128 : (n + 1) * 128]
        return carry

    lax.fori_loop(0, 32, pair, 0, unroll=16)
    v_hi, v_lo = v_ref[0:128, :], v_ref[128:256, :]
    v3 = cat([v_hi, v_hi, v_lo], 0)
    c0 = math.sqrt(2.0 / math.pi)

    def copies(zb, slot):
        out = []
        for n, dst in enumerate((o_ref, t_ref)):
            for h in range(2):
                out.append(pltpu.make_async_copy(
                    out_buf.at[slot * 4 + n * 2 + h], dst.at[:, pl.ds(pl.multiple_of(zb * 8, 8), 8), pl.ds(h * 128, 128)],
                    out_sem.at[slot * 4 + n * 2 + h],
                ))
        return out

    def gather_z(z, slot):
        z16 = z * 16
        u = cat([u_ref[pl.ds(pl.multiple_of(n * 1024 + z16, 16), 16), :] for n in range(8)], 0)
        u_hi, u_lo = split(u.T)
        local = loc_ref[pl.ds(pl.multiple_of(z * 128, 128), 128), :]
        acc_ref[slot] = nn(cat([u_hi, u_lo, u_hi], 1), v3) + local

    take(0).wait()
    gather_z(0, 0)

    def block(zb, carry):
        slot = zb % 2

        @pl.when(zb < 7)
        def _():
            take(zb + 1).wait()

        @pl.when(zb >= 2)
        def _():
            for c in copies(zb, slot):
                c.wait()

        flat = out_buf.reshape(8 * 512, 128)
        for i in range(8):
            gather_z(jnp.minimum(zb * 8 + i + 1, 63), (i + 1) % 2)
            pre = acc_ref[i % 2, 0:64, :]
            tan = acc_ref[i % 2, 64:128, :]
            sq = pre * pre
            t = jnp.tanh(pre * (c0 + (c0 * 0.044715) * sq))
            half = 0.5 + 0.5 * t
            res = pre * half
            slope = half + res * ((1.0 - t) * (c0 + (3.0 * 0.044715 * c0) * sq))
            for n, val in enumerate((res, slope * tan)):
                for h in range(2):
                    flat[pl.ds(slot * 2048 + n * 1024 + h * 512 + i, 64, stride=8), :] = val[:, h * 128 : (h + 1) * 128]
        for c in copies(zb, slot):
            c.start()
        return carry

    lax.fori_loop(0, 8, block, 0)
    for zb in (6, 7):
        for c in copies(zb, zb % 2):
            c.wait()


def inverse(loc, g, v, tz):
    out = jax.ShapeDtypeStruct((64, ZL, FL), F32)
    return pl.pallas_call(
        inverse_kernel,
        out_shape=(out, out),
        in_specs=[HBM, VMEM, VMEM, VMEM],
        out_specs=(HBM, HBM),
        scratch_shapes=[
            pltpu.VMEM((8192, FL), F32), pltpu.VMEM((8192, 128), F32), pltpu.VMEM((2, 128, FL), F32), pltpu.VMEM((8, 64, 8, 128), F32),
            pltpu.SemaphoreType.DMA((8,)), pltpu.SemaphoreType.DMA((8,)),
        ],
        compiler_params=pltpu.CompilerParams(vmem_limit_bytes=VMEM_INVERSE),
        name="inverse_kernel",
    )(loc, g, v, tz)


def body(field, field_tangent, spectral_weight, local_weight, bias_term, z_modes, phi_modes):
    x0 = field.reshape(64, ZL, FL)
    x1 = field_tangent.reshape(64, ZL, FL)
    zm = z_modes.reshape(1, 64)
    pm = phi_modes.reshape(1, 64)
    w = spectral_weight.reshape(2, 16, 16, 2, 2, 8)
    c, o, d, lane = (lax.broadcasted_iota(I32, (16, 16, 16, 128), n) for n in range(4))
    lane_o = lane // 4 % 16
    pick = ((o == lane_o) & (c == (lane_o + d) % 16)).astype(F32)
    wd = jnp.einsum("icokhq,codl->dihkql", w, pick, precision=lax.Precision.HIGHEST).reshape(1024, 128)
    g, loc, v, tz = exchange(x0, x1, pm, zm, wd, local_weight, bias_term.reshape(1, 16))
    out, tan = inverse(loc, g.reshape(8192, 128), v, tz)
    return out.reshape(16, 4, ZL, FL), tan.reshape(16, 4, ZL, FL)


def solution(mesh):
    return jax.shard_map(
        body,
        mesh=mesh,
        in_specs=(
            P(None, None, "gz", "phi"),
            P(None, None, "gz", "phi"),
            P(None, None, None, "gz", "phi"),
            P(),
            P(),
            P(),
            P(),
        ),
        out_specs=(P(None, None, "gz", "phi"), P(None, None, "gz", "phi")),
        check_vma=False,
    )
```

```python
import functools
import math

import jax
import jax.numpy as jnp
from jax import lax
from jax.experimental import pallas as pl
from jax.experimental.pallas import tpu as pltpu
from jax.sharding import PartitionSpec as P

C, R, ZL, FL = 16, 4, 64, 256
Z, PHI, KZ, KP = 2048, 1024, 64, 64
F32, BF16, I32 = jnp.float32, jnp.bfloat16, jnp.int32
MESH = pl.DeviceIdType.MESH
VMEM_EXCHANGE = 46 << 20
VMEM_INVERSE = 44 << 20
SCALE = (1.0 / math.sqrt(Z * PHI)) * (2.0 / math.sqrt(KZ * KP))


def iota(shape, dim):
    return lax.broadcasted_iota(I32, shape, dim)


def split(x):
    hi = x.astype(BF16)
    return hi, (x - hi.astype(F32)).astype(BF16)


def wave(turns, length):
    quarter = length // 4
    near = ((turns + 2 * quarter) & (length - 1)) - 2 * quarter
    x = (quarter - jnp.abs(near)).astype(F32) * (2.0 * math.pi / length)
    x2 = x * x
    acc = 1.0 / math.factorial(13)
    for n in (11, 9, 7, 5, 3, 1):
        acc = acc * x2 + (1.0 if n % 4 == 1 else -1.0) / math.factorial(n)
    return acc * x


def nt(a, b):
    return lax.dot_general(a, b, (((1,), (1,)), ((), ())), preferred_element_type=F32)


def nn(a, b):
    return jnp.dot(a, b, preferred_element_type=F32)


def pick_column(modes_ref, which):
    hit = iota((128, 64), 1) == which
    return jnp.sum(jnp.where(hit, modes_ref[...].astype(F32), 0.0), axis=1, keepdims=True).astype(I32)


def phi_table(modes_ref):
    row = iota((128, 64), 0)
    col = pick_column(modes_ref, row // 16 * 8 + row % 8)
    f = lax.axis_index("phi") * FL + iota((128, FL), 1)
    return wave(f * col + (iota((128, FL), 0) // 8 % 2) * (PHI // 4), PHI)


def z_table(modes_ref, z, turn):
    row = iota((128, 64), 0)
    col = pick_column(modes_ref, row // 4 % 16 * 4 + row // 64 * 2 + row // 2 % 2)
    return wave((lax.axis_index("gz") * ZL + z) * col + turn, Z)


def places(j):
    q = 2 * j
    base = ((q // 16) * 1024 + (q // 8 % 2) * 128 + q % 8, (q // 8) * 128 + q % 8 + 4096)
    step = (256, 1024)
    return [
        [pl.ds(base[g // 8] + (n + (g % 8 // 2) * step[g // 8] + (g % 2) * 64), 8, stride=8) for g in range(16)]
        for n in range(2)
    ]


def fetch(x0_ref, x1_ref, x_buf, sem, zb):
    copies = []
    for p, src in enumerate((x0_ref, x1_ref)):
        for h in range(2):
            n = zb * 4 + p * 2 + h
            copies.append(pltpu.make_async_copy(
                src.at[:, pl.ds(pl.multiple_of(zb * 8, 8), 8), pl.ds(h * 128, 128)], x_buf.at[n], sem.at[n]
            ))
    return copies


def stack_z(x_buf, zb, i):
    flat = x_buf.reshape(32 * 512, 128)
    a, b, c, d = (flat[pl.ds(zb * 2048 + n * 512 + i, 64, stride=8), :] for n in range(4))
    return jnp.concatenate([jnp.concatenate([a, b], axis=1), jnp.concatenate([c, d], axis=1)], axis=0)


def cat(parts, axis):
    return jnp.concatenate(parts, axis=axis)


def transform(x0_ref, x1_ref, pm_ref, zm_ref, s_ref, x_buf, a_ref, xs_ref, v_ref, sem):
    for zb in range(8):
        for c in fetch(x0_ref, x1_ref, x_buf, sem, zb):
            c.start()
    w_hi, w_lo = split(phi_table(pm_ref))
    w2 = cat([w_hi, w_lo], 0)
    v_ref[...] = w2
    shape = (128, 128)
    turn = (iota(shape, 0) % 2 - iota(shape, 1) // 64) * (Z // 4)
    t_hi, t_lo = split(z_table(zm_ref, iota(shape, 1) % 64, turn))
    t3 = cat([t_hi, t_lo, t_hi], 1)

    def arrive(zb):
        for c in fetch(x0_ref, x1_ref, x_buf, sem, zb):
            c.wait()

    def block(k, carry):
        for n in range(2):
            arrive(2 * k + n)
        for i in range(8):
            base = pl.multiple_of(k * 2048, 2048) + i // 4 * 1024
            base2 = pl.multiple_of(k * 4096, 4096) + i * 512
            for n in range(2):
                hi, lo = split(stack_z(x_buf, 2 * k + i // 4, i % 4 * 2 + n))
                xs_ref[pl.ds(base2 + n * 128, 128), :] = hi
                xs_ref[pl.ds(base2 + (256 + n * 128), 128), :] = lo
            hi = xs_ref[pl.ds(base2, 256), :]
            lo = xs_ref[pl.ds(base2 + 256, 256), :]
            o = nt(w2, hi)
            o = o[:128] + (o[128:] + nt(w_hi, lo))
            for n in range(2):
                a_ref[pl.ds(base + (i % 4 * 2 + n), 128, stride=8), :] = o[:, n * 128 : (n + 1) * 128]
        return carry

    lax.fori_loop(0, 4, block, 0)

    def pair(j, carry):
        base = pl.multiple_of(((j // 4) * 16 + j % 4 * 2) * 8, 16)

        def rows(n):
            return cat([
                a_ref[pl.ds(base + (n * 8 + part * 64 + zb * 1024), 8), :] for part in range(2) for zb in range(8)
            ], 0)

        hi, lo = split(cat([rows(0), rows(1)], 1))
        o = nn(t3, cat([hi, hi, lo], 0))
        spots = places(j)
        for n in range(2):
            for g in range(16):
                s_ref[spots[n][g], :] = o[g * 8 : g * 8 + 8, n * 128 : (n + 1) * 128]
        return carry

    lax.fori_loop(0, 32, pair, 0, unroll=16)


def inverse_z(modes_ref, t_ref):
    row, col = iota((128, 128), 0), iota((128, 128), 1)
    turn = (row % 2 - col % 2) * (Z // 4)
    hi, lo = split(z_table(modes_ref, col // 2, turn).T)
    t_ref[:, 0:128] = hi
    t_ref[:, 128:256] = lo


def local_mixing(lw_ref, bias_ref):
    pick = (iota((128, 16), 0) // 4 % 16 == iota((128, 16), 1)).astype(F32)
    full = lax.Precision.HIGHEST
    rows = lax.dot_general(pick, lw_ref[...], (((1,), (1,)), ((), ())), precision=full, preferred_element_type=F32)
    grid = lax.dot_general(rows, pick, (((1,), (1,)), ((), ())), precision=full, preferred_element_type=F32)
    row, col = iota((128, 128), 0), iota((128, 128), 1)
    same = (row // 64 == col // 64) & (row % 4 == col % 4)
    l_hi, l_lo = split(jnp.where(same, grid, 0.0))
    here = (iota((128, 16), 0) // 4 == iota((128, 16), 1))
    bias = jnp.sum(jnp.where(here, bias_ref[...], 0.0), axis=1, keepdims=True)
    return cat([l_hi, l_lo, l_hi], 1), bias


HBM = pl.BlockSpec(memory_space=pltpu.HBM)
VMEM = pl.BlockSpec(memory_space=pltpu.VMEM)


def mix(x_ref, w_ref, out_ref):
    def pair(ref):
        re = cat([ref[pl.ds(n * 16, 8), :] for n in range(4)], 0)
        im = cat([ref[pl.ds(n * 16 + 8, 8), :] for n in range(4)], 0)
        return re * SCALE, im * SCALE

    xr, xi = pair(x_ref)
    lane = iota((32, 128), 1) % 64
    gr = jnp.zeros((32, 128), F32)
    gi = jnp.zeros((32, 128), F32)
    for d in range(16):
        if d == 0:
            ar, ai = xr, xi
        else:
            near = lane < 64 - 4 * d
            ar = jnp.where(near, pltpu.roll(xr, 128 - 4 * d, 1), pltpu.roll(xr, 64 - 4 * d, 1))
            ai = jnp.where(near, pltpu.roll(xi, 128 - 4 * d, 1), pltpu.roll(xi, 64 - 4 * d, 1))
        wr = w_ref[pl.ds(d * 64, 32), :]
        wi = w_ref[pl.ds(d * 64 + 32, 32), :]
        gr = gr + (ar * wr - ai * wi)
        gi = gi + (ai * wr + ar * wi)
    for n in range(4):
        out_ref[pl.ds(n * 16, 8), :] = gr[n * 8 : n * 8 + 8]
        out_ref[pl.ds(n * 16 + 8, 8), :] = gi[n * 8 : n * 8 + 8]


def exchange_kernel(
    x0_ref, x1_ref, pm_ref, zm_ref, w_ref, lw_ref, bias_ref, g_ref, loc_ref, v_ref, t_ref,
    x_buf, a_ref, xs_ref, spec_ref, loc_buf, x_sem, loc_sem, peer, acc, relay, fin, second, relay2, rec2, third, rec3, own, gath3,
    pair_s, pair_r, st1_s, st1_r, st2_s, st2_r, st3_s, st3_r,
    ag3_s, ag3_r, ag2_s, ag2_r, ag1_s, ag1_r, hand_s, hand_r,
):
    gz = lax.axis_index("gz")
    x = lax.axis_index("phi")
    core = gz % 2
    z = (gz // 2) % 4
    y = gz // 8

    def device(xx, yy, zz, cc):
        return ((yy * 4 + zz) * 2 + cc, xx)

    pa = x + core * (y - x)
    pb = z
    pd = y + core * (x - y)

    def along_a(t):
        n = (pa + t) % 4
        return device(n + core * (x - n), y + core * (n - y), z, core)

    def along_b(t):
        return device(x, y, (z + t) % 4, core)

    def along_d(t):
        n = (pd + t) % 4
        return device(x + core * (n - x), n + core * (y - n), z, core)

    partner = device(x, y, z, 1 - core)

    sent = []

    def send(src, dst, ss, rs, dev):
        c = pltpu.make_async_remote_copy(
            src_ref=src, dst_ref=dst, send_sem=ss, recv_sem=rs, device_id=dev, device_id_type=MESH
        )
        c.start()
        sent.append(c)
        return c

    right, left = along_a(1), along_a(3)
    barrier = pltpu.get_barrier_semaphore()
    peers = [partner, right, left]
    peers += [along_b(1), along_b(3)] + [along_d(t) for t in (1, 2, 3)]
    for dev in peers:
        pl.semaphore_signal(barrier, inc=1, device_id=dev, device_id_type=MESH)
    transform(x0_ref, x1_ref, pm_ref, zm_ref, spec_ref, x_buf, a_ref, xs_ref, v_ref, x_sem)
    s_ref = spec_ref.reshape(2, 4, 8, 4, 32, 128)
    pl.semaphore_wait(barrier, 8)

    def mine(t):
        return (pa + t) % 4

    qa = y + core * (x - y)
    order = (2, 1, 3, 0)
    pairs = []
    for n, t in enumerate(order):
        pairs.append(send(s_ref.at[1 - core, (qa + t) % 4], peer.at[n], pair_s.at[n], pair_r.at[n], partner))

    l3, bias = local_mixing(lw_ref, bias_ref)
    stores = []

    def mix_local(zb):
        slot = zb % 2
        if zb >= 2:
            stores[zb - 2].wait()

        def four(i, carry):
            for n in range(4):
                row = (zb * 4 + n // 2) * 512 + n % 2 * 128
                hi = xs_ref[pl.ds(pl.multiple_of(i * 1024 + row, 128), 128), :]
                lo = xs_ref[pl.ds(pl.multiple_of(i * 1024 + row + 256, 128), 128), :]
                o = nn(l3, cat([hi, hi, lo], 0)) + bias
                loc_buf[slot, pl.ds(pl.multiple_of(i * 512 + n * 128, 128), 128), :] = o
            return carry

        lax.fori_loop(0, 2, four, 0)
        c = pltpu.make_async_copy(loc_buf.at[slot], loc_ref.at[pl.ds(zb * 1024, 1024), :], loc_sem.at[zb])
        c.start()
        stores.append(c)

    mix_local(0)

    def land(n):
        pairs[n].wait_recv()
        acc[n] = s_ref[core, mine(order[n])] + peer[n]

    def piece(slab, s, h, size=4):
        return acc.at[slab, pl.ds(h * 4, size), (pb + s) % 4]

    turns = (2, 1, 3, 0)
    land(0)
    relays = {}
    for s in turns:
        n = s * 6
        relays[0, s] = send(piece(0, s, 0), relay.at[0, s], st1_s.at[n], st1_r.at[n], right)
        relays[1, s] = send(piece(0, s, 1), relay.at[1, s], st1_s.at[n + 1], st1_r.at[n + 1], left)
    mix_local(1)
    land(1)
    land(2)
    first = {}
    for s in turns:
        n = s * 6
        first[s] = [
            send(piece(1, s, 1), fin.at[0, s, pl.ds(4, 4)], st1_s.at[n + 2], st1_r.at[n + 2], right),
            send(piece(2, s, 0), fin.at[1, s, pl.ds(0, 4)], st1_s.at[n + 3], st1_r.at[n + 3], left),
        ]
        mix_local(2 + turns.index(s))
        for side, dev in enumerate((right, left)):
            relays[side, s].wait_recv()
            ref = piece(1 + side, s, side)
            ref[...] = ref[...] + relay[side, s]
            dst = fin.at[side, s, pl.ds(side * 4, 4)]
            first[s].append(send(ref, dst, st1_s.at[n + 4 + side], st1_r.at[n + 4 + side], dev))
    land(3)

    sends2 = []
    for s in turns:
        for c in first[s]:
            c.wait_recv()
        second[s] = piece(3, s, 0, 8)[...] + (fin[0, s] + fin[1, s])
        if s == 2:
            far = [
                send(second.at[2, pl.ds(h * 4, 4)], relay2.at[h], st2_s.at[h], st2_r.at[h], along_b(1 + 2 * h))
                for h in range(2)
            ]
        elif s:
            h = s // 2
            far[h].wait_recv()
            part = second.at[s, pl.ds(h * 4, 4)]
            part[...] = part[...] + relay2[h]
            sends2.append(send(second.at[s], rec2.at[h], st2_s.at[2 + h], st2_r.at[2 + h], along_b(s)))
    mix_local(6)
    for c in sends2:
        c.wait_recv()
    third[...] = (second[0] + (rec2[0] + rec2[1])).reshape(4, 64, 128)

    sends3 = []
    for t in turns[:3]:
        sends3.append(send(third.at[(pd + t) % 4], rec3.at[t - 1], st3_s.at[t - 1], st3_r.at[t - 1], along_d(t)))
    mix_local(7)
    for c in sends3:
        c.wait_recv()
    own[...] = third[pd] + rec3[0] + (rec3[1] + rec3[2])
    mine3 = gath3.at[pd]
    mix(own, w_ref, mine3)

    gat3 = [send(mine3, mine3, ag3_s.at[t - 1], ag3_r.at[t - 1], along_d(t)) for t in turns[:3]]
    inverse_z(zm_ref, t_ref)
    for c in gat3:
        c.wait_recv()

    def spot(t, s, h, size=4):
        return g_ref.at[core, mine(t), pl.ds(h * 4, size), (pb + s) % 4]

    mine2 = spot(0, 0, 0, 8)
    mine2[...] = gath3[...].reshape(8, 32, 128)

    gat2, gat1, hands = {}, {}, []

    def pass_b(key, u, h, t):
        n = ("ra", "lb", "rb", "la", "fr", "fl").index(key)
        gat2[key] = send(spot(0, u, h), spot(0, u, h), ag2_s.at[n], ag2_r.at[n], along_b(t))

    def pass_a(key, u, t, h, dev):
        n = u * 6 + ("ra", "lb", "rb", "la", "fr", "fl").index(key)
        gat1[u, key] = send(spot(t, u, h), spot(t, u, h), ag1_s.at[n], ag1_r.at[n], dev)

    def hand(u, n, t, h):
        ref = spot(t, u, h)
        hands.append(send(ref, ref, hand_s.at[u * 8 + n], hand_r.at[u * 8 + n], partner))

    def emit(u, h):
        if h == 0:
            pass_a("ra", u, 0, 0, right)
            pass_a("la", u, 0, 0, left)
        else:
            pass_a("lb", u, 0, 1, left)
            pass_a("rb", u, 0, 1, right)
        hand(u, h, 0, h)

    def turn_round(u):
        gat1[u, "ra"].wait_recv()
        pass_a("fr", u, 3, 0, right)
        gat1[u, "lb"].wait_recv()
        pass_a("fl", u, 1, 1, left)
        hand(u, 2, 3, 0)
        hand(u, 3, 1, 1)

    pass_b("ra", 0, 0, 1)
    pass_b("lb", 0, 1, 3)
    pass_b("rb", 0, 1, 1)
    pass_b("la", 0, 0, 3)
    emit(0, 0)
    emit(0, 1)
    gat2["ra"].wait_recv()
    pass_b("fr", 3, 0, 1)
    gat2["lb"].wait_recv()
    pass_b("fl", 1, 1, 3)
    emit(3, 0)
    emit(1, 1)
    turn_round(0)
    gat2["rb"].wait_recv()
    emit(3, 1)
    gat2["la"].wait_recv()
    emit(1, 0)
    gat2["fr"].wait_recv()
    emit(2, 0)
    gat2["fl"].wait_recv()
    emit(2, 1)
    for u in (3, 1, 2):
        turn_round(u)
    for u in (0, 3, 1, 2):
        gat1[u, "rb"].wait_recv()
        hand(u, 4, 3, 1)
        gat1[u, "la"].wait_recv()
        hand(u, 5, 1, 0)
        gat1[u, "fr"].wait_recv()
        hand(u, 6, 2, 0)
        gat1[u, "fl"].wait_recv()
        hand(u, 7, 2, 1)
    for c in hands:
        c.wait_recv()
    for c in sent:
        c.wait_send()
    for c in stores[6:]:
        c.wait()


def exchange(field, field_tangent, pm, zm, wt, lw, bias):
    dma = pltpu.SemaphoreType.DMA
    buf = lambda *dims: pltpu.VMEM((*dims, 128), F32)
    table = jax.ShapeDtypeStruct((256, 256), BF16)
    return pl.pallas_call(
        exchange_kernel,
        out_shape=(
            jax.ShapeDtypeStruct((2, 4, 8, 4, 32, 128), F32), jax.ShapeDtypeStruct((8192, FL), F32),
            table, jax.ShapeDtypeStruct((128, 256), BF16),
        ),
        in_specs=[HBM, HBM, VMEM, VMEM, VMEM, VMEM, VMEM],
        out_specs=(VMEM, HBM, VMEM, VMEM),
        scratch_shapes=[
            buf(32, 64, 8), buf(8192), pltpu.VMEM((16384, FL), BF16), buf(8192),
            pltpu.VMEM((2, 1024, FL), F32), dma((32,)), dma((8,)),
            buf(4, 8, 4, 32), buf(4, 8, 4, 32), buf(2, 4, 4, 32), buf(2, 4, 8, 32), buf(4, 8, 32), buf(2, 4, 32), buf(2, 8, 32),
            buf(4, 64), buf(3, 64), buf(64), buf(4, 64),
            dma((4,)), dma((4,)), dma((24,)), dma((24,)), dma((4,)), dma((4,)), dma((3,)), dma((3,)),
            dma((3,)), dma((3,)), dma((6,)), dma((6,)), dma((24,)), dma((24,)), dma((32,)), dma((32,)),
        ],
        compiler_params=pltpu.CompilerParams(collective_id=0, has_side_effects=True, vmem_limit_bytes=VMEM_EXCHANGE),
        name="exchange_kernel",
    )(field, field_tangent, pm, zm, wt, lw, bias)


def inverse_kernel(
    loc_hbm, g_ref, v_ref, tz_ref, o_ref, t_ref, loc_ref, u_ref, acc_ref, out_buf, loc_sem, out_sem
):
    def take(zb):
        rows = pl.ds(pl.multiple_of(zb * 1024, 1024), 1024)
        return pltpu.make_async_copy(loc_hbm.at[rows, :], loc_ref.at[rows, :], loc_sem.at[zb])

    for zb in range(8):
        take(zb).start()
    t_hi, t_lo = tz_ref[:, 0:128], tz_ref[:, 128:256]
    t3 = cat([t_hi, t_lo, t_hi], 1)

    def pair(j, carry):
        spots = places(j)
        g2 = cat([cat([g_ref[spots[n][g], :] for g in range(16)], 0) for n in range(2)], 1)
        hi, lo = split(g2)
        o = nn(t3, cat([hi, hi, lo], 0))
        base = (j // 4) * 1024 + j % 4 * 2
        for n in range(2):
            for g in range(16):
                u_ref[pl.ds(base + (n + g * 64), 8, stride=8), :] = o[g * 8 : g * 8 + 8, n * 128 : (n + 1) * 128]
        return carry

    lax.fori_loop(0, 32, pair, 0, unroll=16)
    v_hi, v_lo = v_ref[0:128, :], v_ref[128:256, :]
    v3 = cat([v_hi, v_hi, v_lo], 0)
    c0 = math.sqrt(2.0 / math.pi)

    def copies(zb, slot):
        out = []
        for n, dst in enumerate((o_ref, t_ref)):
            for h in range(2):
                out.append(pltpu.make_async_copy(
                    out_buf.at[slot * 4 + n * 2 + h], dst.at[:, pl.ds(pl.multiple_of(zb * 8, 8), 8), pl.ds(h * 128, 128)],
                    out_sem.at[slot * 4 + n * 2 + h],
                ))
        return out

    def gather_z(z, slot):
        z16 = z * 16
        u = cat([u_ref[pl.ds(pl.multiple_of(n * 1024 + z16, 16), 16), :] for n in range(8)], 0)
        u_hi, u_lo = split(u.T)
        local = loc_ref[pl.ds(pl.multiple_of(z * 128, 128), 128), :]
        acc_ref[slot] = nn(cat([u_hi, u_lo, u_hi], 1), v3) + local

    take(0).wait()
    gather_z(0, 0)

    def block(k, carry):
        take(2 * k + 1).wait()

        @pl.when(k < 3)
        def _():
            take(2 * k + 2).wait()

        @pl.when(k >= 2)
        def _():
            for n in range(2):
                for c in copies(2 * k + n, k % 2 * 2 + n):
                    c.wait()

        flat = out_buf.reshape(16 * 512, 128)
        for n2 in range(2):
            zb = 2 * k + n2
            slot = k % 2 * 2 + n2
            for i in range(8):
                gather_z(jnp.minimum(zb * 8 + i + 1, 63), (i + 1) % 2)
                pre = acc_ref[i % 2, 0:64, :]
                tan = acc_ref[i % 2, 64:128, :]
                sq = pre * pre
                t = jnp.tanh(pre * (c0 + (c0 * 0.044715) * sq))
                half = 0.5 + 0.5 * t
                res = pre * half
                slope = half + res * ((1.0 - t) * (c0 + (3.0 * 0.044715 * c0) * sq))
                for n, val in enumerate((res, slope * tan)):
                    for h in range(2):
                        flat[pl.ds(slot * 2048 + n * 1024 + h * 512 + i, 64, stride=8), :] = val[:, h * 128 : (h + 1) * 128]
            for c in copies(zb, slot):
                c.start()
        return carry

    lax.fori_loop(0, 4, block, 0)
    for zb in (4, 5, 6, 7):
        for c in copies(zb, zb % 4):
            c.wait()


def inverse(loc, g, v, tz):
    out = jax.ShapeDtypeStruct((64, ZL, FL), F32)
    return pl.pallas_call(
        inverse_kernel,
        out_shape=(out, out),
        in_specs=[HBM, VMEM, VMEM, VMEM],
        out_specs=(HBM, HBM),
        scratch_shapes=[
            pltpu.VMEM((8192, FL), F32), pltpu.VMEM((8192, 128), F32), pltpu.VMEM((2, 128, FL), F32), pltpu.VMEM((16, 64, 8, 128), F32),
            pltpu.SemaphoreType.DMA((8,)), pltpu.SemaphoreType.DMA((16,)),
        ],
        compiler_params=pltpu.CompilerParams(vmem_limit_bytes=VMEM_INVERSE),
        name="inverse_kernel",
    )(loc, g, v, tz)


def body(field, field_tangent, spectral_weight, local_weight, bias_term, z_modes, phi_modes):
    x0 = field.reshape(64, ZL, FL)
    x1 = field_tangent.reshape(64, ZL, FL)
    zm = z_modes.reshape(1, 64)
    pm = phi_modes.reshape(1, 64)
    w = spectral_weight.reshape(2, 16, 16, 2, 2, 8)
    c, o, d, lane = (lax.broadcasted_iota(I32, (16, 16, 16, 128), n) for n in range(4))
    lane_o = lane // 4 % 16
    pick = ((o == lane_o) & (c == (lane_o + d) % 16)).astype(F32)
    wd = jnp.einsum("icokhq,codl->dihkql", w, pick, precision=lax.Precision.HIGHEST).reshape(1024, 128)
    g, loc, v, tz = exchange(x0, x1, pm, zm, wd, local_weight, bias_term.reshape(1, 16))
    out, tan = inverse(loc, g.reshape(8192, 128), v, tz)
    return out.reshape(16, 4, ZL, FL), tan.reshape(16, 4, ZL, FL)


def solution(mesh):
    return jax.shard_map(
        body,
        mesh=mesh,
        in_specs=(
            P(None, None, "gz", "phi"),
            P(None, None, "gz", "phi"),
            P(None, None, None, "gz", "phi"),
            P(),
            P(),
            P(),
            P(),
        ),
        out_specs=(P(None, None, "gz", "phi"), P(None, None, "gz", "phi")),
        check_vma=False,
    )
```
